1024 devices in a mesh: dp: 8 (over y), ctx: 32 (over z_hi, x, core), tp: 4 (over z_lo).
Axes of the slice: x: 4, y: 8, z: 16 (z_hi: 4, z_lo: 4; z = z_hi * 4 + z_lo), core: 2. Of those that a mesh axis runs over, the one named last changes fastest.
Arguments:
- queries: bfloat16 [32768, 4096], P(('dp', 'ctx'), 'tp'), parts along dimension 0, may hold values from -6.5 to 6.5
- keys: bfloat16 [32768, 512], P(('dp', 'ctx'), 'tp'), parts along dimension 0, may hold values from -6.5 to 6.5
- values: bfloat16 [32768, 512], P(('dp', 'ctx'), 'tp'), parts along dimension 0, may hold values from -6 to 6
- out_weight: bfloat16 [4096, 2048], P('tp'), may hold values from -0.375 to 0.375
- norm_gain: float32 [2048], replicated, may hold values from 0.5 to 1.5
- expert_gate: bfloat16 [128, 2048, 384], P(('ctx', 'tp')), may hold values from -0.125 to 0.125
- expert_up: bfloat16 [128, 2048, 384], P(('ctx', 'tp')), may hold values from -0.125 to 0.125
- expert_down: bfloat16 [128, 384, 2048], P(('ctx', 'tp')), may hold values from -0.3125 to 0.3125
- expert_ids: int32 [32768, 8], P(('dp', 'ctx')), parts along dimension 0, may hold values from 0 to 127, as said below
- route_weights: float32 [32768, 8], P(('dp', 'ctx')), parts along dimension 0, may hold values from 0.05 to 1
Outputs:
- attended: bfloat16 [32768, 4096], P(('dp', 'ctx'), 'tp'), parts along dimension 0
- layer_out: bfloat16 [32768, 2048], P(('dp', 'ctx', 'tp')), parts along dimension 0
The draws below stay inside these ranges and needn't reach their ends.
There are 8 independent parts, one for each index of `dp`. The reference program is written for one: setup_inputs(seed, part) draws one part's arguments, and reference() takes and returns one part's arrays. A program takes and returns all parts, laid end to end along the dimension named above; an argument that names none is the same for every part. Nothing has to cross between parts.
Inputs may be any that keep to these rules, and one draw needn't show every extreme that they name: `expert_ids`: each row names 8 different experts. In each aligned block of 128 rows (the rows of one ctx index) every expert is named by at least 4 and at most 12 rows, and one expert is named by exactly 12 rows in every block.
All inputs are finite; a program needn't handle non-finite values.
Results may differ from the reference program's by a relative error of at most 0.02.
Values may be sent and summed in bfloat16 or wider, within the bound.
A program may use at most 64 MiB of HBM per device.

```python
import jax
import jax.numpy as jnp
from jax import lax

D = 2048
QH = 32
KVH = 4
HEAD = 128
TOPK = 8
EFF = 384
BLK = 128
L = 4096
EXPERTS = 128
CAP = 12
N_CTX = 32


def base_field(key, features):
    return jnp.clip(jax.random.normal(key, (L, features), jnp.float32), -6.0, 6.0)


def draw_queries(key, part):
    field = base_field(jax.random.fold_in(key, 11), QH * HEAD).reshape(L, QH, HEAD)
    return field.reshape(L, QH * HEAD).astype(jnp.bfloat16)


def draw_keys(key, part):
    field = base_field(jax.random.fold_in(key, 12), KVH * HEAD).reshape(L, KVH, HEAD)
    return field.reshape(L, KVH * HEAD).astype(jnp.bfloat16)


def route_block(key, hot_expert):
    base_load = BLK * TOPK // EXPERTS
    spread_load = CAP - base_load
    ranking = jax.random.permutation(jax.random.fold_in(key, 1), EXPERTS).astype(jnp.int32)
    ranking = jnp.where(jnp.arange(EXPERTS, dtype=jnp.int32) == hot_expert, -1, ranking)
    pairing = jnp.argsort(ranking, stable=True)
    moves = jax.random.randint(jax.random.fold_in(key, 2), (EXPERTS // 2,), 0, spread_load + 1)
    moves = moves.at[0].set(spread_load)
    loads = jnp.full((EXPERTS,), base_load, jnp.int32).at[pairing[0::2]].add(moves).at[pairing[1::2]].add(-moves)
    layout = jax.random.permutation(jax.random.fold_in(key, 3), EXPERTS).astype(jnp.int32)
    ends = jnp.cumsum(loads[layout])
    entries = jnp.arange(BLK * TOPK, dtype=jnp.int32)
    owner = jnp.sum((ends[None, :] <= entries[:, None]).astype(jnp.int32), axis=1)
    block_table = layout[owner].reshape(TOPK, BLK).T
    row_order = jax.random.permutation(jax.random.fold_in(key, 4), BLK)
    return block_table[row_order]


def draw_expert_ids(key, part):
    hot_expert = jax.random.randint(jax.random.fold_in(key, 21), (), 0, EXPERTS)
    block_keys = jax.random.split(jax.random.fold_in(key, 22), L // BLK)
    blocks = jax.vmap(lambda one_key: route_block(one_key, hot_expert))(block_keys)
    return blocks.reshape(L, TOPK).astype(jnp.int32)


def shard_levels(stream_key, extent, pieces, least, top_value):
    gain, own = 1.0, jax.random.fold_in(stream_key, 6)
    for position, blocks in pieces:
        heights = jnp.exp(jax.random.uniform(jax.random.fold_in(own, position), (blocks,), jnp.float32, least / len(pieces), top_value / len(pieces)))
        gain = gain * jnp.repeat(heights, extent[position] // blocks).reshape([-1 if axis == position else 1 for axis in range(len(extent))])
    return gain


def normal_values(stream_key, dims, scale, most, shards=(), kind=jnp.bfloat16):
    level = shard_levels(stream_key, dims, shards, -0.22, 0.18) if shards else 1.0
    result = jax.random.normal(stream_key, dims, jnp.float32) * scale * level
    return jnp.minimum(jnp.maximum(result, -most), most).astype(kind)


def setup_inputs(seed: int = 0, part: int = 0) -> dict:
    key_list = jax.random.split(jax.random.key(seed), 11)
    part_keys = jax.random.split(jax.random.fold_in(key_list[10], part), 11)
    queries = draw_queries(jax.random.fold_in(jax.random.fold_in(key_list[10], part), 71), part)
    keys = draw_keys(jax.random.fold_in(jax.random.fold_in(key_list[10], part), 71), part)
    values = normal_values(part_keys[2], (L, KVH * HEAD), 1.0, 6.0, ((0, 32), (1, 4)))
    out_weight = normal_values(key_list[3], (QH * HEAD, D), (QH * HEAD // 16) ** -0.5, 0.375, ((0, 4),))
    norm_gain = jnp.clip(1.0 + 0.1 * jax.random.normal(key_list[4], (D,), jnp.float32), 0.5, 1.5)
    expert_gate = normal_values(key_list[5], (EXPERTS, D, EFF), D ** -0.5, 0.125, ((0, 128),))
    expert_up = normal_values(key_list[6], (EXPERTS, D, EFF), D ** -0.5, 0.125, ((0, 128),))
    expert_down = normal_values(key_list[7], (EXPERTS, EFF, D), EFF ** -0.5, 0.3125, ((0, 128),))
    expert_ids = draw_expert_ids(jax.random.fold_in(jax.random.fold_in(key_list[10], part), 71), part)
    route_weights = jnp.clip(0.05 + 0.95 * jax.random.uniform(part_keys[9], (L, TOPK), jnp.float32) ** shard_levels(part_keys[9], (L, TOPK), ((0, 32),), -0.2, 0.2), 0.05, 1.0)
    return {"queries": queries, "keys": keys, "values": values, "out_weight": out_weight, "norm_gain": norm_gain, "expert_gate": expert_gate, "expert_up": expert_up, "expert_down": expert_down, "expert_ids": expert_ids, "route_weights": route_weights}


def head_attention(operands):
    q_head, k_head, v_head = operands
    scores = jnp.dot(q_head, k_head.T, preferred_element_type=jnp.float32) * HEAD ** (-0.5)
    positions = jnp.arange(L, dtype=jnp.int32)
    allowed = positions[None, :] <= positions[:, None]
    scores = jnp.where(allowed, scores, -jnp.inf)
    row_max = lax.optimization_barrier(jnp.max(scores, axis=1, keepdims=True))
    probs = jnp.exp(scores - row_max)
    row_total = lax.optimization_barrier(jnp.sum(probs, axis=1, keepdims=True))
    weighted = jnp.dot(probs.astype(jnp.bfloat16), v_head, preferred_element_type=jnp.float32)
    return (weighted / row_total).astype(jnp.bfloat16)

def reference(queries, keys, values, out_weight, norm_gain, expert_gate, expert_up, expert_down, expert_ids, route_weights):
    group_size = QH // KVH
    q_heads = queries.reshape(L, QH, HEAD).transpose(1, 0, 2)
    k_heads = jnp.repeat(keys.reshape(L, KVH, HEAD).transpose(1, 0, 2), group_size, axis=0)
    v_heads = jnp.repeat(values.reshape(L, KVH, HEAD).transpose(1, 0, 2), group_size, axis=0)
    attended_heads = lax.map(head_attention, (q_heads, k_heads, v_heads))
    attended = attended_heads.transpose(1, 0, 2).reshape(L, QH * HEAD)
    projected = jnp.dot(attended, out_weight, preferred_element_type=jnp.float32)
    normed = (projected * lax.rsqrt(lax.optimization_barrier(jnp.mean(projected * projected, axis=1, keepdims=True)) + 1e-06) * norm_gain).astype(jnp.bfloat16)
    share = route_weights / lax.optimization_barrier(jnp.sum(route_weights, axis=1, keepdims=True))
    flat_ids = expert_ids.reshape(-1).astype(jnp.int32)
    token_index = (jnp.arange(L * TOPK, dtype=jnp.int32) // TOPK).astype(jnp.int32)
    one_hot = (flat_ids[:, None] == jnp.arange(EXPERTS, dtype=jnp.int32)[None, :]).astype(jnp.int32)
    running = jnp.cumsum(one_hot, axis=0).astype(jnp.int32) - 1
    slot_index = lax.optimization_barrier(jnp.sum(running * one_hot, axis=1)).astype(jnp.int32)
    max_load = N_CTX * CAP
    slot_table = jnp.zeros((EXPERTS, max_load), jnp.int32).at[flat_ids, slot_index].set(token_index)

    def run_expert(operands):
        gate_weight, up_weight, down_weight, token_rows = operands
        inputs = normed[token_rows]
        gate_proj = jnp.dot(inputs, gate_weight, preferred_element_type=jnp.float32)
        up_proj = jnp.dot(inputs, up_weight, preferred_element_type=jnp.float32)
        activated = (jax.nn.silu(gate_proj) * up_proj).astype(jnp.bfloat16)
        return jnp.dot(activated, down_weight, preferred_element_type=jnp.float32).astype(jnp.bfloat16)
    expert_outs = lax.map(run_expert, (expert_gate, expert_up, expert_down, slot_table))
    assigned = expert_outs[flat_ids, slot_index].astype(jnp.float32).reshape(L, TOPK, D)
    expert_mix = lax.optimization_barrier(jnp.sum(assigned * share[:, :, None], axis=1))
    layer_out = (projected + expert_mix).astype(jnp.bfloat16)
    return (attended, layer_out)
```

```python
import math

import jax
import jax.numpy as jnp
from jax import lax
from jax.experimental import pallas as pl
from jax.experimental.pallas import tpu as pltpu
from jax.sharding import PartitionSpec as P

MESH = pl.DeviceIdType.MESH
BF16 = jnp.bfloat16
F32 = jnp.float32
HEAD = 128
HEADS = 8
BLK = 128
D = 2048
EFF = 384
ROWS = 32
SLOTS = 16
NEG = -1e30


def layer_kernel(
    q_hbm, k_hbm, v_hbm, w_hbm, gain_hbm, gate_hbm, up_hbm, down_hbm, route_hbm,
    att_hbm, out_hbm,
    q_v, q_h, kv, w_v, gain_v, gate_v, up_v, down_v, route,
    m_s, l_s, acc_s, att_v, proj_f, rs_s, rs_r, proj_own,
    dmap, mmap, xg, xs, xr, ys, ret, contrib, sp, sm, rp, rm, out_v,
    load_sem, send_sem, kv_sem, route_sem, rs_sem, agp_sem, agm_sem, xd_sem, xb_sem, rp_sem, rm_sem, self_sem,
):
    ctx = lax.axis_index("ctx")
    tp = lax.axis_index("tp")
    zh = ctx // 8
    row = ctx % 8
    x = row // 2
    core = ctx % 2
    z = zh * 4 + tp

    sends = []

    def send(src, dst, recv_sem, device):
        copy = pltpu.make_async_remote_copy(
            src_ref=src, dst_ref=dst, send_sem=send_sem.at[len(sends)], recv_sem=recv_sem,
            device_id=device, device_id_type=MESH,
        )
        copy.start()
        sends.append(copy)

    def arrived(dst, recv_sem):
        pltpu.make_async_remote_copy(
            src_ref=dst, dst_ref=dst, send_sem=send_sem.at[0], recv_sem=recv_sem,
            device_id=at_row(row), device_id_type=MESH,
        ).wait_recv()

    def at_zh(z_hi):
        return {"ctx": z_hi * 8 + row, "tp": tp}

    def at_row(r):
        return {"ctx": zh * 8 + r, "tp": tp}

    def at_z(zz):
        return {"ctx": (zz // 4) * 8 + row, "tp": zz % 4}

    def at_tp(t):
        return {"ctx": ctx, "tp": t}

    def zmod(offset):
        return (z + offset + 16) % 16

    loads = {}

    def load(name, src, dst):
        copy = pltpu.make_async_copy(src, dst, load_sem.at[len(loads)])
        copy.start()
        loads[name] = copy

    load("k", k_hbm, kv.at[ctx, pl.ds(0, BLK)])
    load("v", v_hbm, kv.at[ctx, pl.ds(BLK, BLK)])
    load("route", route_hbm, route.at[zh])
    load("q", q_hbm, q_v)
    load("w", w_hbm, w_v)
    load("gain", gain_hbm, gain_v)
    load("gate", gate_hbm, gate_v)
    load("up", up_hbm, up_v)
    load("down", down_hbm, down_v)

    barrier = pltpu.get_barrier_semaphore()
    partners = [at_zh((zh + d) % 4) for d in (1, 2, 3)]
    partners += [at_row((row + o) % 8) for o in range(1, 8)]
    partners += [at_tp((tp + o) % 4) for o in (1, 2, 3)]
    partners += [at_z(zmod(1)), at_z(zmod(-1))]
    for partner in partners:
        pl.semaphore_signal(barrier, inc=1, device_id=partner, device_id_type=MESH)
    pl.semaphore_wait(barrier, len(partners))

    sibling = row + 1 - 2 * core
    loads["k"].wait()
    loads["v"].wait()

    def send_block(block, device):
        send(kv.at[block], kv.at[block], kv_sem.at[block], device)

    def x_row(dx):
        return ((x + dx) % 4) * 2 + core

    for d in (2, 1, 3):
        send_block(ctx, at_zh((zh + d) % 4))
    for dx in (2, 1, 3):
        send_block(ctx, at_row(x_row(dx)))
    send_block(ctx, at_row(sibling))
    loads["route"].wait()
    for d in (1, 2, 3):
        send(route.at[zh], route.at[zh], route_sem.at[zh], at_zh((zh + d) % 4))

    loads["q"].wait()
    for h in range(HEADS):
        q_h[h] = q_v[:, h * HEAD : (h + 1) * HEAD]

    score_scale = (HEAD**-0.5) * math.log2(math.e)

    def attend(s, first):
        def head(h, carry):
            keys = kv[pl.ds(s * 8, 8), 0:BLK, :].reshape(8 * BLK, HEAD)
            vals = kv[pl.ds(s * 8, 8), BLK : 2 * BLK, :].reshape(8 * BLK, HEAD)
            scores = lax.dot_general(
                q_h[h], keys, (((1,), (1,)), ((), ())), preferred_element_type=F32
            )
            scores = scores * score_scale
            if first:
                key_pos = lax.broadcasted_iota(jnp.int32, scores.shape, 1)
                query_pos = lax.broadcasted_iota(jnp.int32, scores.shape, 0) + row * BLK
                scores = jnp.where(key_pos <= query_pos, scores, NEG)
            top = jnp.max(scores, axis=1, keepdims=True)
            if first:
                new_max = jnp.broadcast_to(top, (BLK, HEAD))
            else:
                new_max = jnp.maximum(m_s[h], top)
            weights = [
                jnp.exp2(scores[:, j * HEAD : (j + 1) * HEAD] - new_max) for j in range(8)
            ]
            total = weights[0]
            for j in range(1, 8):
                total = total + weights[j]
            update = jnp.dot(
                jnp.concatenate([w.astype(BF16) for w in weights], axis=1),
                vals,
                preferred_element_type=F32,
            )
            if first:
                l_s[h] = total
                acc_s[h] = update
            else:
                rescale = jnp.exp2(m_s[h] - new_max)
                l_s[h] = l_s[h] * rescale + total
                acc_s[h] = acc_s[h] * rescale + update
            m_s[h] = new_max
            return carry

        lax.fori_loop(0, HEADS, head, 0)

    def collect(s):
        for dx in (1, 3, 2):
            block = s * 8 + x_row(dx)
            arrived(kv.at[block], kv_sem.at[block])
            send_block(block, at_row(sibling))
        for dx in (0, 1, 3, 2):
            block = s * 8 + ((x + dx) % 4) * 2 + 1 - core
            arrived(kv.at[block], kv_sem.at[block])

    collect(zh)
    attend(zh, True)

    for d in (1, 3, 2):
        block = ((zh + d) % 4) * 8 + row
        arrived(kv.at[block], kv_sem.at[block])
        for dx in (2, 1, 3):
            send_block(block, at_row(x_row(dx)))
        send_block(block, at_row(sibling))

    for d in (1, 2, 3):
        src = (zh + d) % 4
        arrived(route.at[src], route_sem.at[src])
    earlier = (
        lax.broadcasted_iota(jnp.int32, (BLK, BLK), 0)
        < lax.broadcasted_iota(jnp.int32, (BLK, BLK), 1)
    ).astype(F32).astype(BF16)
    slot = lax.broadcasted_iota(jnp.int32, (SLOTS, BLK), 0).astype(F32)
    for b in range(4):
        ids = route[b, 0:8, :]
        share = route[b, 8:16, :]
        share = share / jnp.sum(share, axis=0, keepdims=True)
        hits, picked = [], []
        for r in range(8):
            same = ids == (zh * 32 + tp + 4 * r).astype(F32)
            hits.append(jnp.sum(jnp.where(same, 1.0, 0.0), axis=0, keepdims=True))
            picked.append(jnp.sum(jnp.where(same, share, 0.0), axis=0, keepdims=True))
        hit = jnp.concatenate(hits, axis=0)
        rank = jnp.dot(hit.astype(BF16), earlier, preferred_element_type=F32)
        choose = [
            jnp.where(slot == rank[r : r + 1], hit[r : r + 1], 0.0) for r in range(8)
        ]
        dmap[b] = jnp.concatenate(choose, axis=0).astype(BF16)
        back = jnp.concatenate([choose[r] * picked[r] for r in range(8)], axis=0)
        mmap[b] = back.T.astype(BF16)

    for d in (3, 1, 2):
        s = (zh + d) % 4
        collect(s)

        @pl.when(s < zh)
        def _():
            attend(s, False)

    for h in range(HEADS):
        att_v[:, h * HEAD : (h + 1) * HEAD] = (
            acc_s[h] / jnp.sum(l_s[h], axis=1, keepdims=True)
        ).astype(BF16)
    att_store = pltpu.make_async_copy(att_v, att_hbm, self_sem.at[8])
    att_store.start()

    loads["w"].wait()
    for half in range(2):
        for n in range(2):
            cols = pl.ds(half * 1024 + n * 512, 512)
            part = jnp.dot(att_v[...], w_v[:, cols], preferred_element_type=F32)
            proj_f[:, cols] = part
            rs_s[:, cols] = part.astype(BF16)
        cols = pl.ds(half * 1024, 1024)
        for o in (2, 1, 3):
            owner = (tp + o) % 4
            send(
                rs_s.at[pl.ds(pl.multiple_of(owner * ROWS, ROWS), ROWS), cols],
                rs_r.at[o - 1, :, cols],
                rs_sem.at[half, o - 1],
                at_tp(owner),
            )
    loads["gain"].wait()
    for half in range(2):
        cols = pl.ds(half * 1024, 1024)
        for o in (2, 1, 3):
            arrived(rs_r.at[o - 1, :, cols], rs_sem.at[half, o - 1])
    own_rows = pl.ds(pl.multiple_of(tp * ROWS, ROWS), ROWS)
    projected = (
        proj_f[own_rows, :] + rs_r[0].astype(F32) + rs_r[1].astype(F32) + rs_r[2].astype(F32)
    )
    proj_own[...] = projected
    inverse = lax.rsqrt(jnp.mean(projected * projected, axis=1, keepdims=True) + 1e-06)
    xg[zh, own_rows, :] = (projected * inverse * gain_v[...]).astype(BF16)

    def piece(origin, half):
        start = pl.multiple_of((origin % 4) * ROWS + half * 16, 16)
        return xg.at[origin // 4, pl.ds(start, 16)]

    def ring_step(k):
        for half in range(2):
            if k > 1:
                arrived(piece(zmod(1 - k), half), agp_sem.at[half, k - 2])
            here = piece(zmod(1 - k), half)
            send(here, here, agp_sem.at[half, k - 1], at_z(zmod(1)))
            if k > 1:
                arrived(piece(zmod(k - 1), half), agm_sem.at[half, k - 2])
            if k <= 7:
                here = piece(zmod(k - 1), half)
                send(here, here, agm_sem.at[half, k - 1], at_z(zmod(-1)))

    def ring_end():
        for half in range(2):
            arrived(piece(zmod(-8), half), agp_sem.at[half, 7])

    side = 2 * (tp // 2) - 1
    order = [zh, (zh + side + 4) % 4, (zh - side + 4) % 4, (zh + 2) % 4]
    own_slots = pl.ds(pl.multiple_of(row * SLOTS, SLOTS), SLOTS)
    local = {}

    def exchange(src, dst, sems, i, n):
        for o in (4, 5, 3, 2, 6, 7, 1):
            r = (row + o) % 8
            slots = pl.ds(pl.multiple_of(r * SLOTS, SLOTS), SLOTS)
            send(src.at[i, slots], dst.at[i, own_slots], sems.at[i, o], at_row(r))
        copy = pltpu.make_async_copy(
            src.at[i, own_slots], dst.at[i, own_slots], self_sem.at[n]
        )
        copy.start()
        local[n] = copy

    def exchanged(dst, sems, i, copy):
        for o in range(1, 8):
            r = (row - o + 8) % 8
            slots = pl.ds(pl.multiple_of(r * SLOTS, SLOTS), SLOTS)
            arrived(dst.at[i, slots], sems.at[i, o])
        copy.wait()

    def dispatch(i):
        for n in range(4):
            cols = pl.ds(n * 512, 512)
            xs[i, :, cols] = jnp.dot(
                dmap[order[i]], xg[order[i], :, cols], preferred_element_type=F32
            ).astype(BF16)
        exchange(xs, xr, xd_sem, i, i)

    def expert(i):
        exchanged(xr, xd_sem, i, local[i])
        items = xr[i]
        gate = jnp.dot(items, gate_v[...], preferred_element_type=F32)
        up = jnp.dot(items, up_v[...], preferred_element_type=F32)
        act = (gate / (1.0 + jnp.exp(-gate)) * up).astype(BF16)
        for n in range(4):
            cols = pl.ds(n * 512, 512)
            ys[i, :, cols] = jnp.dot(
                act, down_v[:, cols], preferred_element_type=F32
            ).astype(BF16)
        exchange(ys, ret, xb_sem, i, 4 + i)

    def mix(i):
        exchanged(ret, xb_sem, i, local[4 + i])
        for n in range(4):
            cols = pl.ds(n * 512, 512)
            contrib[order[i], :, cols] = jnp.dot(
                mmap[order[i]], ret[i, :, cols], preferred_element_type=F32
            )

    for k in (1, 2, 3, 4):
        ring_step(k)
    dispatch(0)
    for k in (5, 6):
        ring_step(k)
    dispatch(1)
    for k in (7, 8):
        ring_step(k)
    dispatch(2)
    loads["gate"].wait()
    loads["up"].wait()
    loads["down"].wait()
    expert(0)
    ring_end()
    dispatch(3)
    expert(1)
    expert(2)
    expert(3)
    mix(0)
    mix(1)
    mix(2)
    mix(3)

    def term(dest, half):
        start = pl.multiple_of((dest % 4) * ROWS + half * 16, 16)
        return contrib[dest // 4, pl.ds(start, 16), :]

    for k in range(1, 9):
        for half in range(2):
            rows = pl.ds(half * 16, 16)
            total = term(zmod(9 - k), half)
            if k > 1:
                arrived(rp.at[k - 2, rows], rp_sem.at[half, k - 2])
                total = total + rp[k - 2, rows].astype(F32)
            sp[k - 1, rows] = total.astype(BF16)
            send(sp.at[k - 1, rows], rp.at[k - 1, rows], rp_sem.at[half, k - 1], at_z(zmod(1)))
            if k <= 7:
                total = term(zmod(k - 8), half)
                if k > 1:
                    arrived(rm.at[k - 2, rows], rm_sem.at[half, k - 2])
                    total = total + rm[k - 2, rows].astype(F32)
                sm[k - 1, rows] = total.astype(BF16)
                send(
                    sm.at[k - 1, rows], rm.at[k - 1, rows], rm_sem.at[half, k - 1], at_z(zmod(-1))
                )
    for half in range(2):
        rows = pl.ds(half * 16, 16)
        arrived(rm.at[6, rows], rm_sem.at[half, 6])
        arrived(rp.at[7, rows], rp_sem.at[half, 7])
        out_v[rows] = (
            proj_own[rows]
            + term(z, half)
            + rp[7, rows].astype(F32)
            + rm[6, rows].astype(F32)
        ).astype(BF16)
    out_store = pltpu.make_async_copy(out_v, out_hbm, self_sem.at[9])
    out_store.start()
    for copy in sends:
        copy.wait_send()
    att_store.wait()
    out_store.wait()


def per_device(
    queries, keys, values, out_weight, norm_gain,
    expert_gate, expert_up, expert_down, expert_ids, route_weights,
):
    route = jnp.concatenate([expert_ids.astype(F32), route_weights], axis=1).T
    any_spec = pl.BlockSpec(memory_space=pl.ANY)
    vmem = pltpu.VMEM
    dma = pltpu.SemaphoreType.DMA
    return pl.pallas_call(
        layer_kernel,
        out_shape=(
            jax.ShapeDtypeStruct((BLK, HEADS * HEAD), BF16),
            jax.ShapeDtypeStruct((ROWS, D), BF16),
        ),
        in_specs=[any_spec] * 9,
        out_specs=(any_spec, any_spec),
        scratch_shapes=[
            vmem((BLK, HEADS * HEAD), BF16),
            vmem((HEADS, BLK, HEAD), BF16),
            vmem((32, 2 * BLK, HEAD), BF16),
            vmem((HEADS * HEAD, D), BF16),
            vmem((1, D), F32),
            vmem((D, EFF), BF16),
            vmem((D, EFF), BF16),
            vmem((EFF, D), BF16),
            vmem((4, 16, BLK), F32),
            vmem((HEADS, BLK, HEAD), F32),
            vmem((HEADS, BLK, HEAD), F32),
            vmem((HEADS, BLK, HEAD), F32),
            vmem((BLK, HEADS * HEAD), BF16),
            vmem((BLK, D), F32),
            vmem((BLK, D), BF16),
            vmem((3, ROWS, D), BF16),
            vmem((ROWS, D), F32),
            vmem((4, 8 * SLOTS, BLK), BF16),
            vmem((4, BLK, 8 * SLOTS), BF16),
            vmem((4, BLK, D), BF16),
            vmem((4, 8 * SLOTS, D), BF16),
            vmem((4, 8 * SLOTS, D), BF16),
            vmem((4, 8 * SLOTS, D), BF16),
            vmem((4, 8 * SLOTS, D), BF16),
            vmem((4, BLK, D), F32),
            vmem((8, ROWS, D), BF16),
            vmem((7, ROWS, D), BF16),
            vmem((8, ROWS, D), BF16),
            vmem((7, ROWS, D), BF16),
            vmem((ROWS, D), BF16),
            dma((9,)),
            dma((180,)),
            dma((32,)),
            dma((4,)),
            dma((2, 3)),
            dma((2, 8)),
            dma((2, 7)),
            dma((4, 8)),
            dma((4, 8)),
            dma((2, 8)),
            dma((2, 7)),
            dma((10,)),
        ],
        compiler_params=pltpu.CompilerParams(
            collective_id=0, has_side_effects=True, vmem_limit_bytes=60 * 1024 * 1024
        ),
        name="layer",
    )(
        queries, keys, values, out_weight, norm_gain.reshape(1, D),
        expert_gate.reshape(D, EFF), expert_up.reshape(D, EFF), expert_down.reshape(EFF, D), route,
    )


def solution(mesh):
    in_specs = (
        P(("dp", "ctx"), "tp"),
        P(("dp", "ctx"), "tp"),
        P(("dp", "ctx"), "tp"),
        P("tp", None),
        P(),
        P(("ctx", "tp"), None, None),
        P(("ctx", "tp"), None, None),
        P(("ctx", "tp"), None, None),
        P(("dp", "ctx"), None),
        P(("dp", "ctx"), None),
    )
    out_specs = (P(("dp", "ctx"), "tp"), P(("dp", "ctx", "tp"), None))
    return jax.shard_map(
        per_device, mesh=mesh, in_specs=in_specs, out_specs=out_specs, check_vma=False
    )
```

```python
import math

import jax
import jax.numpy as jnp
from jax import lax
from jax.experimental import pallas as pl
from jax.experimental.pallas import tpu as pltpu
from jax.sharding import PartitionSpec as P

MESH = pl.DeviceIdType.MESH
BF16 = jnp.bfloat16
F32 = jnp.float32
HEAD = 128
HEADS = 8
BLK = 128
D = 2048
EFF = 384
ROWS = 32
SLOTS = 16
NEG = -1e30


def layer_kernel(
    q_hbm, k_hbm, v_hbm, w_hbm, gain_hbm, gate_hbm, up_hbm, down_hbm, ids_hbm, share_hbm,
    att_hbm, out_hbm,
    q_v, q_h, kv, w_v, gain_v, gate_v, up_v, down_v, ids_v, share_v, route,
    m_s, l_s, acc_s, att_v, proj_f, rs_s, rs_r, proj_own,
    dmap, mmap, xg, xs, xr, ys, ret, contrib, sp, sm, rp, rm, out_v,
    load_sem, send_sem, kv_sem, route_sem, rs_sem, agp_sem, agm_sem, xd_sem, xb_sem, rp_sem, rm_sem, self_sem,
):
    ctx = lax.axis_index("ctx")
    tp = lax.axis_index("tp")
    zh = ctx // 8
    row = ctx % 8
    x = row // 2
    core = ctx % 2
    z = zh * 4 + tp

    sends = []

    def send(src, dst, recv_sem, device):
        copy = pltpu.make_async_remote_copy(
            src_ref=src, dst_ref=dst, send_sem=send_sem.at[len(sends)], recv_sem=recv_sem,
            device_id=device, device_id_type=MESH,
        )
        copy.start()
        sends.append(copy)

    def arrived(dst, recv_sem):
        pltpu.make_async_remote_copy(
            src_ref=dst, dst_ref=dst, send_sem=send_sem.at[0], recv_sem=recv_sem,
            device_id=at_row(row), device_id_type=MESH,
        ).wait_recv()

    def at_zh(z_hi):
        return {"ctx": z_hi * 8 + row, "tp": tp}

    def at_row(r):
        return {"ctx": zh * 8 + r, "tp": tp}

    def at_z(zz):
        return {"ctx": (zz // 4) * 8 + row, "tp": zz % 4}

    def at_tp(t):
        return {"ctx": ctx, "tp": t}

    def zmod(offset):
        return (z + offset + 16) % 16

    loads = {}

    def load(name, src, dst):
        copy = pltpu.make_async_copy(src, dst, load_sem.at[len(loads)])
        copy.start()
        loads[name] = copy

    load("k", k_hbm, kv.at[ctx, pl.ds(0, BLK)])
    load("v", v_hbm, kv.at[ctx, pl.ds(BLK, BLK)])
    load("ids", ids_hbm, ids_v)
    load("share", share_hbm, share_v)
    load("q", q_hbm, q_v)
    load("w", w_hbm, w_v)
    load("gain", gain_hbm, gain_v)
    load("gate", gate_hbm, gate_v)
    load("up", up_hbm, up_v)
    load("down", down_hbm, down_v)

    barrier = pltpu.get_barrier_semaphore()
    partners = [at_zh((zh + d) % 4) for d in (1, 3)]
    partners += [at_row((row + o) % 8) for o in range(1, 8)]
    partners += [at_tp((tp + o) % 4) for o in (1, 2, 3)]
    above, below = at_z(zmod(1)), at_z(zmod(-1))
    partners += [above, below]
    for partner in partners:
        pl.semaphore_signal(barrier, inc=1, device_id=partner, device_id_type=MESH)

    loads["ids"].wait()
    loads["share"].wait()
    route[zh, 0:8, :] = ids_v[...].astype(F32)
    route[zh, 8:16, :] = share_v[...]
    loads["q"].wait()
    for h in range(HEADS):
        q_h[h] = q_v[:, h * HEAD : (h + 1) * HEAD]

    pl.semaphore_wait(barrier, len(partners))

    sibling = row + 1 - 2 * core
    loads["k"].wait()
    loads["v"].wait()

    def send_block(block, device):
        send(kv.at[block], kv.at[block], kv_sem.at[block], device)

    def x_row(dx):
        return ((x + dx) % 4) * 2 + core

    for d in (1, 3):
        send_block(ctx, at_zh((zh + d) % 4))
    for dx in (2, 1, 3):
        send_block(ctx, at_row(x_row(dx)))
    send_block(ctx, at_row(sibling))
    for d in (1, 3):
        send(route.at[zh], route.at[zh], route_sem.at[zh], at_zh((zh + d) % 4))

    score_scale = (HEAD**-0.5) * math.log2(math.e)

    def attend(s, first):
        def head(h, carry):
            keys = kv[pl.ds(s * 8, 8), 0:BLK, :].reshape(8 * BLK, HEAD)
            vals = kv[pl.ds(s * 8, 8), BLK : 2 * BLK, :].reshape(8 * BLK, HEAD)
            scores = lax.dot_general(
                q_h[h], keys, (((1,), (1,)), ((), ())), preferred_element_type=F32
            )
            scores = scores * score_scale
            if first:
                key_pos = lax.broadcasted_iota(jnp.int32, scores.shape, 1)
                query_pos = lax.broadcasted_iota(jnp.int32, scores.shape, 0) + row * BLK
                scores = jnp.where(key_pos <= query_pos, scores, NEG)
            top = jnp.max(scores, axis=1, keepdims=True)
            if first:
                new_max = jnp.broadcast_to(top, (BLK, HEAD))
            else:
                new_max = jnp.maximum(m_s[h], top)
            weights = [
                jnp.exp2(scores[:, j * HEAD : (j + 1) * HEAD] - new_max) for j in range(8)
            ]
            total = weights[0]
            for j in range(1, 8):
                total = total + weights[j]
            update = jnp.dot(
                jnp.concatenate([w.astype(BF16) for w in weights], axis=1),
                vals,
                preferred_element_type=F32,
            )
            if first:
                l_s[h] = total
                acc_s[h] = update
            else:
                rescale = jnp.exp2(m_s[h] - new_max)
                l_s[h] = l_s[h] * rescale + total
                acc_s[h] = acc_s[h] * rescale + update
            m_s[h] = new_max
            return carry

        lax.fori_loop(0, HEADS, head, 0)

    def collect(s):
        for dx in (1, 3, 2):
            block = s * 8 + x_row(dx)
            arrived(kv.at[block], kv_sem.at[block])
            send_block(block, at_row(sibling))
        for dx in (0, 1, 3, 2):
            block = s * 8 + ((x + dx) % 4) * 2 + 1 - core
            arrived(kv.at[block], kv_sem.at[block])

    collect(zh)
    attend(zh, True)

    def spread(block):
        for dx in (2, 1, 3):
            send_block(block, at_row(x_row(dx)))
        send_block(block, at_row(sibling))

    for d in (3, 1):
        block = ((zh + d) % 4) * 8 + row
        arrived(kv.at[block], kv_sem.at[block])
    send_block(((zh + 3 + 2 * core) % 4) * 8 + row, at_zh((zh + 1 + 2 * core) % 4))
    for d in (3, 1):
        spread(((zh + d) % 4) * 8 + row)
    for d in (3, 1):
        src = (zh + d) % 4
        arrived(route.at[src], route_sem.at[src])
    src = (zh + 3) % 4
    send(route.at[src], route.at[src], route_sem.at[src], at_zh((zh + 1) % 4))

    def attend_earlier(d):
        s = (zh + d) % 4
        collect(s)

        @pl.when(s < zh)
        def _():
            attend(s, False)

    attend_earlier(3)
    block = ((zh + 2) % 4) * 8 + row
    arrived(kv.at[block], kv_sem.at[block])
    spread(block)
    attend_earlier(1)

    src = (zh + 2) % 4
    arrived(route.at[src], route_sem.at[src])
    earlier = (
        lax.broadcasted_iota(jnp.int32, (BLK, BLK), 0)
        < lax.broadcasted_iota(jnp.int32, (BLK, BLK), 1)
    ).astype(F32).astype(BF16)
    slot = lax.broadcasted_iota(jnp.int32, (SLOTS, BLK), 0).astype(F32)
    for b in range(4):
        ids = route[b, 0:8, :]
        share = route[b, 8:16, :]
        share = share / jnp.sum(share, axis=0, keepdims=True)
        hits, picked = [], []
        for r in range(8):
            same = ids == (zh * 32 + tp + 4 * r).astype(F32)
            hits.append(jnp.sum(jnp.where(same, 1.0, 0.0), axis=0, keepdims=True))
            picked.append(jnp.sum(jnp.where(same, share, 0.0), axis=0, keepdims=True))
        hit = jnp.concatenate(hits, axis=0)
        rank = jnp.dot(hit.astype(BF16), earlier, preferred_element_type=F32)
        choose = [
            jnp.where(slot == rank[r : r + 1], hit[r : r + 1], 0.0) for r in range(8)
        ]
        dmap[b] = jnp.concatenate(choose, axis=0).astype(BF16)
        back = jnp.concatenate([choose[r] * picked[r] for r in range(8)], axis=0)
        mmap[b] = back.T.astype(BF16)

    attend_earlier(2)

    for h in range(HEADS):
        att_v[:, h * HEAD : (h + 1) * HEAD] = (
            acc_s[h] / jnp.sum(l_s[h], axis=1, keepdims=True)
        ).astype(BF16)
    att_store = pltpu.make_async_copy(att_v, att_hbm, self_sem.at[8])
    att_store.start()

    loads["w"].wait()
    for n in range(4):
        cols = pl.ds(n * 512, 512)
        part = jnp.dot(att_v[...], w_v[:, cols], preferred_element_type=F32)
        proj_f[:, cols] = part
        rs_s[:, cols] = part.astype(BF16)
        for o in (2, 1, 3):
            owner = (tp + o) % 4
            send(
                rs_s.at[pl.ds(pl.multiple_of(owner * ROWS, ROWS), ROWS), cols],
                rs_r.at[o - 1, :, cols],
                rs_sem.at[n, o - 1],
                at_tp(owner),
            )
    loads["gain"].wait()
    for n in range(4):
        cols = pl.ds(n * 512, 512)
        for o in (2, 1, 3):
            arrived(rs_r.at[o - 1, :, cols], rs_sem.at[n, o - 1])
    own_rows = pl.ds(pl.multiple_of(tp * ROWS, ROWS), ROWS)
    projected = (
        proj_f[own_rows, :] + rs_r[0].astype(F32) + rs_r[1].astype(F32) + rs_r[2].astype(F32)
    )
    proj_own[...] = projected
    inverse = lax.rsqrt(jnp.mean(projected * projected, axis=1, keepdims=True) + 1e-06)
    xg[z] = (projected * inverse * gain_v[...]).astype(BF16)

    def piece(origin, n):
        return xg.at[origin, :, pl.ds(n * 512, 512)]

    def ring_step(k):
        for n in range(4):
            here = piece(zmod(1 - k), n)
            if k > 1:
                arrived(here, agp_sem.at[n, k - 2])
            send(here, here, agp_sem.at[n, k - 1], above)
            here = piece(zmod(k - 1), n)
            if k > 1:
                arrived(here, agm_sem.at[n, k - 2])
            if k <= 7:
                send(here, here, agm_sem.at[n, k - 1], below)

    def ring_end():
        for n in range(4):
            arrived(piece(zmod(-8), n), agp_sem.at[n, 7])

    side = 2 * (tp // 2) - 1
    order = [zh, (zh + side + 4) % 4, (zh - side + 4) % 4, (zh + 2) % 4]
    own_slots = pl.ds(pl.multiple_of(row * SLOTS, SLOTS), SLOTS)
    local = {}

    def exchange(src, dst, sems, i, n):
        for o in (4, 5, 3, 2, 6, 7, 1):
            r = (row + o) % 8
            slots = pl.ds(pl.multiple_of(r * SLOTS, SLOTS), SLOTS)
            send(src.at[i, slots], dst.at[i, own_slots], sems.at[i, o], at_row(r))
        copy = pltpu.make_async_copy(
            src.at[i, own_slots], dst.at[i, own_slots], self_sem.at[n]
        )
        copy.start()
        local[n] = copy

    def exchanged(dst, sems, i, copy):
        for o in range(1, 8):
            r = (row - o + 8) % 8
            slots = pl.ds(pl.multiple_of(r * SLOTS, SLOTS), SLOTS)
            arrived(dst.at[i, slots], sems.at[i, o])
        copy.wait()

    def dispatch(i):
        for n in range(4):
            cols = pl.ds(n * 512, 512)
            xs[i, :, cols] = jnp.dot(
                dmap[order[i]],
                xg[pl.ds(order[i] * 4, 4), :, cols].reshape(BLK, 512),
                preferred_element_type=F32,
            ).astype(BF16)
        exchange(xs, xr, xd_sem, i, i)

    def expert(i):
        exchanged(xr, xd_sem, i, local[i])
        items = xr[i]
        gate = jnp.dot(items, gate_v[...], preferred_element_type=F32)
        up = jnp.dot(items, up_v[...], preferred_element_type=F32)
        act = (gate / (1.0 + jnp.exp(-gate)) * up).astype(BF16)
        for n in range(4):
            cols = pl.ds(n * 512, 512)
            ys[i, :, cols] = jnp.dot(
                act, down_v[:, cols], preferred_element_type=F32
            ).astype(BF16)
        exchange(ys, ret, xb_sem, i, 4 + i)

    def mix(i):
        exchanged(ret, xb_sem, i, local[4 + i])
        for n in range(4):
            cols = pl.ds(n * 512, 512)
            contrib[pl.ds(order[i] * 4, 4), :, cols] = jnp.dot(
                mmap[order[i]], ret[i, :, cols], preferred_element_type=F32
            ).reshape(4, ROWS, 512)

    for k in (1, 2, 3, 4):
        ring_step(k)
    dispatch(0)
    for k in (5, 6):
        ring_step(k)
    dispatch(1)
    ring_step(7)
    loads["gate"].wait()
    loads["up"].wait()
    loads["down"].wait()
    expert(0)
    ring_step(8)
    dispatch(2)
    expert(1)
    ring_end()
    dispatch(3)
    expert(2)
    mix(0)
    mix(1)
    expert(3)
    mix(2)
    mix(3)

    for k in range(1, 9):
        for n in range(4):
            cols = pl.ds(n * 512, 512)
            total = contrib[zmod(9 - k), :, cols]
            if k > 1:
                arrived(rp.at[k - 2, :, cols], rp_sem.at[n, k - 2])
                total = total + rp[k - 2, :, cols].astype(F32)
            sp[k - 1, :, cols] = total.astype(BF16)
            send(sp.at[k - 1, :, cols], rp.at[k - 1, :, cols], rp_sem.at[n, k - 1], above)
            if k <= 7:
                total = contrib[zmod(k - 8), :, cols]
                if k > 1:
                    arrived(rm.at[k - 2, :, cols], rm_sem.at[n, k - 2])
                    total = total + rm[k - 2, :, cols].astype(F32)
                sm[k - 1, :, cols] = total.astype(BF16)
                send(sm.at[k - 1, :, cols], rm.at[k - 1, :, cols], rm_sem.at[n, k - 1], below)
    for n in range(4):
        cols = pl.ds(n * 512, 512)
        arrived(rm.at[6, :, cols], rm_sem.at[n, 6])
        arrived(rp.at[7, :, cols], rp_sem.at[n, 7])
        out_v[:, cols] = (
            proj_own[:, cols]
            + contrib[z, :, cols]
            + rp[7, :, cols].astype(F32)
            + rm[6, :, cols].astype(F32)
        ).astype(BF16)
    out_store = pltpu.make_async_copy(out_v, out_hbm, self_sem.at[9])
    out_store.start()
    for copy in sends:
        copy.wait_send()
    att_store.wait()
    out_store.wait()


def per_device(
    queries, keys, values, out_weight, norm_gain,
    expert_gate, expert_up, expert_down, expert_ids, route_weights,
):
    any_spec = pl.BlockSpec(memory_space=pl.ANY)
    vmem = pltpu.VMEM
    dma = pltpu.SemaphoreType.DMA
    return pl.pallas_call(
        layer_kernel,
        out_shape=(
            jax.ShapeDtypeStruct((BLK, HEADS * HEAD), BF16),
            jax.ShapeDtypeStruct((ROWS, D), BF16),
        ),
        in_specs=[any_spec] * 10,
        out_specs=(any_spec, any_spec),
        scratch_shapes=[
            vmem((BLK, HEADS * HEAD), BF16),
            vmem((HEADS, BLK, HEAD), BF16),
            vmem((32, 2 * BLK, HEAD), BF16),
            vmem((HEADS * HEAD, D), BF16),
            vmem((1, D), F32),
            vmem((D, EFF), BF16),
            vmem((D, EFF), BF16),
            vmem((EFF, D), BF16),
            vmem((8, BLK), jnp.int32),
            vmem((8, BLK), F32),
            vmem((4, 16, BLK), F32),
            vmem((HEADS, BLK, HEAD), F32),
            vmem((HEADS, BLK, HEAD), F32),
            vmem((HEADS, BLK, HEAD), F32),
            vmem((BLK, HEADS * HEAD), BF16),
            vmem((BLK, D), F32),
            vmem((BLK, D), BF16),
            vmem((3, ROWS, D), BF16),
            vmem((ROWS, D), F32),
            vmem((4, 8 * SLOTS, BLK), BF16),
            vmem((4, BLK, 8 * SLOTS), BF16),
            vmem((16, ROWS, D), BF16),
            vmem((4, 8 * SLOTS, D), BF16),
            vmem((4, 8 * SLOTS, D), BF16),
            vmem((4, 8 * SLOTS, D), BF16),
            vmem((4, 8 * SLOTS, D), BF16),
            vmem((16, ROWS, D), F32),
            vmem((8, ROWS, D), BF16),
            vmem((7, ROWS, D), BF16),
            vmem((8, ROWS, D), BF16),
            vmem((7, ROWS, D), BF16),
            vmem((ROWS, D), BF16),
            dma((10,)),
            dma((256,)),
            dma((32,)),
            dma((4,)),
            dma((4, 3)),
            dma((4, 8)),
            dma((4, 7)),
            dma((4, 8)),
            dma((4, 8)),
            dma((4, 8)),
            dma((4, 7)),
            dma((10,)),
        ],
        compiler_params=pltpu.CompilerParams(
            collective_id=0, has_side_effects=True, vmem_limit_bytes=60 * 1024 * 1024
        ),
        name="layer",
    )(
        queries, keys, values, out_weight, norm_gain.reshape(1, D),
        expert_gate.reshape(D, EFF), expert_up.reshape(D, EFF), expert_down.reshape(EFF, D),
        expert_ids.T, route_weights.T,
    )


def solution(mesh):
    in_specs = (
        P(("dp", "ctx"), "tp"),
        P(("dp", "ctx"), "tp"),
        P(("dp", "ctx"), "tp"),
        P("tp", None),
        P(),
        P(("ctx", "tp"), None, None),
        P(("ctx", "tp"), None, None),
        P(("ctx", "tp"), None, None),
        P(("dp", "ctx"), None),
        P(("dp", "ctx"), None),
    )
    out_specs = (P(("dp", "ctx"), "tp"), P(("dp", "ctx", "tp"), None))
    return jax.shard_map(
        per_device, mesh=mesh, in_specs=in_specs, out_specs=out_specs, check_vma=False
    )
```

```python
import math

import jax
import jax.numpy as jnp
from jax import lax
from jax.experimental import pallas as pl
from jax.experimental.pallas import tpu as pltpu
from jax.sharding import PartitionSpec as P

MESH = pl.DeviceIdType.MESH
BF16 = jnp.bfloat16
F32 = jnp.float32
HEAD = 128
HEADS = 8
BLK = 128
D = 2048
EFF = 384
ROWS = 32
SLOTS = 16
CHUNKS = 16
WIDE = D // CHUNKS
NEG = -1e30


def layer_kernel(
    q_hbm, k_hbm, v_hbm, w_hbm, gain_hbm, gate_hbm, up_hbm, down_hbm, ids_hbm, share_hbm,
    att_v, out_v,
    q_v, q_h, kv, w_v, gain_v, gate_v, up_v, down_v, ids_v, share_v, route,
    m_s, l_s, acc_s, proj_f, rs_s, rs_r, proj_own,
    dmap, mmap, xg, xs, xr, ys, ret, contrib, sp, sm, rp, rm,
    load_sem, send_sem, ring_send, kv_sem, kvz_sem, route_sem, rs_sem, agp_sem, agm_sem, xd_sem, xb_sem, rp_sem, rm_sem, self_sem,
):
    ctx = lax.axis_index("ctx")
    tp = lax.axis_index("tp")
    zh = ctx // 8
    row = ctx % 8
    x = row // 2
    core = ctx % 2
    z = zh * 4 + tp

    sends = []

    def send(src, dst, recv_sem, device):
        copy = pltpu.make_async_remote_copy(
            src_ref=src, dst_ref=dst, send_sem=send_sem.at[len(sends)], recv_sem=recv_sem,
            device_id=device, device_id_type=MESH,
        )
        copy.start()
        sends.append(copy)

    def arrived(dst, recv_sem):
        pltpu.make_async_remote_copy(
            src_ref=dst, dst_ref=dst, send_sem=send_sem.at[0], recv_sem=recv_sem,
            device_id=at_row(row), device_id_type=MESH,
        ).wait_recv()

    def at_zh(z_hi):
        return {"ctx": z_hi * 8 + row, "tp": tp}

    def at_row(r):
        return {"ctx": zh * 8 + r, "tp": tp}

    def at_z(zz):
        return {"ctx": (zz // 4) * 8 + row, "tp": zz % 4}

    def at_tp(t):
        return {"ctx": ctx, "tp": t}

    def zmod(offset):
        return (z + offset + 16) % 16

    loads = {}

    def load(name, src, dst):
        copy = pltpu.make_async_copy(src, dst, load_sem.at[len(loads)])
        copy.start()
        loads[name] = copy

    load("k", k_hbm, kv.at[ctx, pl.ds(0, BLK)])
    load("v", v_hbm, kv.at[ctx, pl.ds(BLK, BLK)])
    load("ids", ids_hbm, ids_v)
    load("share", share_hbm, share_v)
    load("q", q_hbm, q_v)
    load("w", w_hbm, w_v)
    load("gain", gain_hbm, gain_v)
    load("gate", gate_hbm, gate_v)
    load("up", up_hbm, up_v)
    load("down", down_hbm, down_v)

    barrier = pltpu.get_barrier_semaphore()
    partners = [at_zh((zh + d) % 4) for d in (1, 3)]
    partners += [at_row((row + o) % 8) for o in range(1, 8)]
    partners += [at_tp((tp + o) % 4) for o in (1, 2, 3)]
    above, below = at_z(zmod(1)), at_z(zmod(-1))
    partners += [above, below]
    for partner in partners:
        pl.semaphore_signal(barrier, inc=1, device_id=partner, device_id_type=MESH)

    loads["ids"].wait()
    loads["share"].wait()
    route[zh, 0:8, :] = ids_v[...].astype(F32)
    route[zh, 8:16, :] = share_v[...]
    loads["q"].wait()
    for h in range(HEADS):
        q_h[h] = q_v[:, h * HEAD : (h + 1) * HEAD]

    pl.semaphore_wait(barrier, len(partners))

    sibling = row + 1 - 2 * core
    loads["k"].wait()
    loads["v"].wait()

    def send_block(block, device):
        send(kv.at[block], kv.at[block], kv_sem.at[block], device)

    def x_row(dx):
        return ((x + dx) % 4) * 2 + core

    def half_block(z_hi, half):
        return kv.at[z_hi * 8 + row, pl.ds(half * BLK, BLK)]

    for half in range(2):
        for d in (1, 3):
            here = half_block(zh, half)
            send(here, here, kvz_sem.at[zh, half], at_zh((zh + d) % 4))
    for dx in (2, 1, 3):
        send_block(ctx, at_row(x_row(dx)))
    send_block(ctx, at_row(sibling))
    for d in (1, 3):
        send(route.at[zh], route.at[zh], route_sem.at[zh], at_zh((zh + d) % 4))

    score_scale = (HEAD**-0.5) * math.log2(math.e)

    def attend(s, first):
        def head(h, carry):
            keys = kv[pl.ds(s * 8, 8), 0:BLK, :].reshape(8 * BLK, HEAD)
            vals = kv[pl.ds(s * 8, 8), BLK : 2 * BLK, :].reshape(8 * BLK, HEAD)
            scores = lax.dot_general(
                q_h[h], keys, (((1,), (1,)), ((), ())), preferred_element_type=F32
            )
            scores = scores * score_scale
            if first:
                key_pos = lax.broadcasted_iota(jnp.int32, scores.shape, 1)
                query_pos = lax.broadcasted_iota(jnp.int32, scores.shape, 0) + row * BLK
                scores = jnp.where(key_pos <= query_pos, scores, NEG)
            top = jnp.max(scores, axis=1, keepdims=True)
            if first:
                new_max = jnp.broadcast_to(top, (BLK, HEAD))
            else:
                new_max = jnp.maximum(m_s[h], top)
            weights = [
                jnp.exp2(scores[:, j * HEAD : (j + 1) * HEAD] - new_max) for j in range(8)
            ]
            total = weights[0]
            for j in range(1, 8):
                total = total + weights[j]
            update = jnp.dot(
                jnp.concatenate([w.astype(BF16) for w in weights], axis=1),
                vals,
                preferred_element_type=F32,
            )
            if first:
                l_s[h] = total
                acc_s[h] = update
            else:
                rescale = jnp.exp2(m_s[h] - new_max)
                l_s[h] = l_s[h] * rescale + total
                acc_s[h] = acc_s[h] * rescale + update
            m_s[h] = new_max
            return carry

        lax.fori_loop(0, HEADS, head, 0)

    def collect(s):
        for dx in (1, 3, 2):
            block = s * 8 + x_row(dx)
            arrived(kv.at[block], kv_sem.at[block])
            send_block(block, at_row(sibling))
        for dx in (0, 1, 3, 2):
            block = s * 8 + ((x + dx) % 4) * 2 + 1 - core
            arrived(kv.at[block], kv_sem.at[block])

    collect(zh)
    attend(zh, True)

    def spread(block):
        for dx in (2, 1, 3):
            send_block(block, at_row(x_row(dx)))
        send_block(block, at_row(sibling))

    passed = (zh + 3 + 2 * core) % 4
    other = (zh + 1 + 2 * core) % 4
    for half in range(2):
        here = half_block(passed, half)
        arrived(here, kvz_sem.at[passed, half])
        send(here, here, kvz_sem.at[passed, half], at_zh(other))
    for half in range(2):
        arrived(half_block(other, half), kvz_sem.at[other, half])
    for d in (3, 1):
        spread(((zh + d) % 4) * 8 + row)
    for d in (3, 1):
        src = (zh + d) % 4
        arrived(route.at[src], route_sem.at[src])
    src = (zh + 3) % 4
    send(route.at[src], route.at[src], route_sem.at[src], at_zh((zh + 1) % 4))

    def attend_earlier(d):
        s = (zh + d) % 4
        collect(s)

        @pl.when(s < zh)
        def _():
            attend(s, False)

    attend_earlier(3)
    far = (zh + 2) % 4
    for half in range(2):
        arrived(half_block(far, half), kvz_sem.at[far, half])
    spread(far * 8 + row)
    attend_earlier(1)

    src = (zh + 2) % 4
    arrived(route.at[src], route_sem.at[src])
    earlier = (
        lax.broadcasted_iota(jnp.int32, (BLK, BLK), 0)
        < lax.broadcasted_iota(jnp.int32, (BLK, BLK), 1)
    ).astype(F32).astype(BF16)
    slot = lax.broadcasted_iota(jnp.int32, (SLOTS, BLK), 0).astype(F32)
    for b in range(4):
        ids = route[b, 0:8, :]
        share = route[b, 8:16, :]
        share = share / jnp.sum(share, axis=0, keepdims=True)
        hits, picked = [], []
        for r in range(8):
            same = ids == (zh * 32 + tp + 4 * r).astype(F32)
            hits.append(jnp.sum(jnp.where(same, 1.0, 0.0), axis=0, keepdims=True))
            picked.append(jnp.sum(jnp.where(same, share, 0.0), axis=0, keepdims=True))
        hit = jnp.concatenate(hits, axis=0)
        rank = jnp.dot(hit.astype(BF16), earlier, preferred_element_type=F32)
        choose = [
            jnp.where(slot == rank[r : r + 1], hit[r : r + 1], 0.0) for r in range(8)
        ]
        dmap[b] = jnp.concatenate(choose, axis=0).astype(BF16)
        back = jnp.concatenate([choose[r] * picked[r] for r in range(8)], axis=0)
        mmap[b] = back.T.astype(BF16)

    attend_earlier(2)

    for h in range(HEADS):
        att_v[:, h * HEAD : (h + 1) * HEAD] = (
            acc_s[h] / jnp.sum(l_s[h], axis=1, keepdims=True)
        ).astype(BF16)

    loads["w"].wait()
    for n in range(4):
        cols = pl.ds(n * 512, 512)
        part = jnp.dot(att_v[...], w_v[:, cols], preferred_element_type=F32)
        proj_f[:, cols] = part
        rs_s[:, cols] = part.astype(BF16)
        for o in (2, 1, 3):
            owner = (tp + o) % 4
            send(
                rs_s.at[pl.ds(pl.multiple_of(owner * ROWS, ROWS), ROWS), cols],
                rs_r.at[o - 1, :, cols],
                rs_sem.at[n, o - 1],
                at_tp(owner),
            )
    loads["gain"].wait()
    for n in range(4):
        cols = pl.ds(n * 512, 512)
        for o in (2, 1, 3):
            arrived(rs_r.at[o - 1, :, cols], rs_sem.at[n, o - 1])
    own_rows = pl.ds(pl.multiple_of(tp * ROWS, ROWS), ROWS)
    projected = (
        proj_f[own_rows, :] + rs_r[0].astype(F32) + rs_r[1].astype(F32) + rs_r[2].astype(F32)
    )
    proj_own[...] = projected
    inverse = lax.rsqrt(jnp.mean(projected * projected, axis=1, keepdims=True) + 1e-06)
    normed = (projected * inverse * gain_v[...]).astype(BF16)
    for j in range(CHUNKS):
        xg[z, j] = normed[:, j * WIDE : (j + 1) * WIDE]

    def pass_on(src, dst, sems, send_at, j, k, device):
        pltpu.make_async_remote_copy(
            src_ref=src, dst_ref=dst, send_sem=ring_send.at[send_at], recv_sem=sems.at[j, k - 1],
            device_id=device, device_id_type=MESH,
        ).start()

    def ring_step(k):
        def chunk(j, carry):
            here = xg.at[zmod(1 - k), j]
            if k > 1:
                arrived(here, agp_sem.at[j, k - 2])
            pass_on(here, here, agp_sem, 0, j, k, above)
            here = xg.at[zmod(k - 1), j]
            if k > 1:
                arrived(here, agm_sem.at[j, k - 2])
            if k <= 7:
                pass_on(here, here, agm_sem, 0, j, k, below)
            return carry

        lax.fori_loop(0, CHUNKS, chunk, 0)

    def ring_end():
        def chunk(j, carry):
            arrived(xg.at[zmod(-8), j], agp_sem.at[j, 7])
            return carry

        lax.fori_loop(0, CHUNKS, chunk, 0)

    side = 2 * (tp // 2) - 1
    order = [zh, (zh + side + 4) % 4, (zh - side + 4) % 4, (zh + 2) % 4]
    own_slots = pl.ds(pl.multiple_of(row * SLOTS, SLOTS), SLOTS)
    local = {}

    def exchange(src, dst, sems, i, n):
        for o in (4, 5, 3, 2, 6, 7, 1):
            r = (row + o) % 8
            slots = pl.ds(pl.multiple_of(r * SLOTS, SLOTS), SLOTS)
            send(src.at[i, slots], dst.at[i, own_slots], sems.at[i, o], at_row(r))
        copy = pltpu.make_async_copy(
            src.at[i, own_slots], dst.at[i, own_slots], self_sem.at[n]
        )
        copy.start()
        local[n] = copy

    def exchanged(dst, sems, i, copy):
        for o in range(1, 8):
            r = (row - o + 8) % 8
            slots = pl.ds(pl.multiple_of(r * SLOTS, SLOTS), SLOTS)
            arrived(dst.at[i, slots], sems.at[i, o])
        copy.wait()

    def dispatch(i):
        for n in range(4):
            cols = pl.ds(n * 512, 512)
            tokens = [
                xg[pl.ds(order[i] * 4, 4), j].reshape(BLK, WIDE)
                for j in range(n * 512 // WIDE, (n + 1) * 512 // WIDE)
            ]
            xs[i, :, cols] = jnp.dot(
                dmap[order[i]], jnp.concatenate(tokens, axis=1), preferred_element_type=F32
            ).astype(BF16)
        exchange(xs, xr, xd_sem, i, i)

    def expert(i):
        exchanged(xr, xd_sem, i, local[i])
        items = xr[i]
        gate = jnp.dot(items, gate_v[...], preferred_element_type=F32)
        up = jnp.dot(items, up_v[...], preferred_element_type=F32)
        act = (gate / (1.0 + jnp.exp(-gate)) * up).astype(BF16)
        for n in range(4):
            cols = pl.ds(n * 512, 512)
            ys[i, :, cols] = jnp.dot(
                act, down_v[:, cols], preferred_element_type=F32
            ).astype(BF16)
        exchange(ys, ret, xb_sem, i, 4 + i)

    def mix(i):
        exchanged(ret, xb_sem, i, local[4 + i])
        for n in range(4):
            cols = pl.ds(n * 512, 512)
            mixed = jnp.dot(mmap[order[i]], ret[i, :, cols], preferred_element_type=F32)
            for j in range(512 // WIDE):
                contrib[pl.ds(order[i] * 4, 4), n * 512 // WIDE + j] = mixed[
                    :, j * WIDE : (j + 1) * WIDE
                ].reshape(4, ROWS, WIDE)

    for k in (1, 2, 3, 4):
        ring_step(k)
    dispatch(0)
    for k in (5, 6):
        ring_step(k)
    dispatch(1)
    ring_step(7)
    loads["gate"].wait()
    loads["up"].wait()
    loads["down"].wait()
    expert(0)
    ring_step(8)
    dispatch(2)
    expert(1)
    ring_end()
    dispatch(3)
    expert(2)
    mix(0)
    mix(1)
    expert(3)
    mix(2)
    mix(3)

    def scatter_step(k):
        def chunk(j, carry):
            total = contrib[zmod(9 - k), j]
            if k > 1:
                arrived(rp.at[k - 2, j], rp_sem.at[j, k - 2])
                total = total + rp[k - 2, j].astype(F32)
            sp[k - 1, j] = total.astype(BF16)
            pass_on(sp.at[k - 1, j], rp.at[k - 1, j], rp_sem, 1, j, k, above)
            if k <= 7:
                total = contrib[zmod(k - 8), j]
                if k > 1:
                    arrived(rm.at[k - 2, j], rm_sem.at[j, k - 2])
                    total = total + rm[k - 2, j].astype(F32)
                sm[k - 1, j] = total.astype(BF16)
                pass_on(sm.at[k - 1, j], rm.at[k - 1, j], rm_sem, 2, j, k, below)
            return carry

        lax.fori_loop(0, CHUNKS, chunk, 0)

    for k in range(1, 9):
        scatter_step(k)
    for j in range(CHUNKS):
        cols = pl.ds(j * WIDE, WIDE)
        arrived(rm.at[6, j], rm_sem.at[j, 6])
        arrived(rp.at[7, j], rp_sem.at[j, 7])
        out_v[:, cols] = (
            proj_own[:, cols]
            + contrib[z, j]
            + rp[7, j].astype(F32)
            + rm[6, j].astype(F32)
        ).astype(BF16)
    for i, sent in enumerate((xg.at[pl.ds(0, 15)], sp, sm)):
        pltpu.make_async_remote_copy(
            src_ref=sent, dst_ref=sent, send_sem=ring_send.at[i], recv_sem=ring_send.at[i],
            device_id=above, device_id_type=MESH,
        ).wait_send()
    for copy in sends:
        copy.wait_send()


def per_device(
    queries, keys, values, out_weight, norm_gain,
    expert_gate, expert_up, expert_down, expert_ids, route_weights,
):
    hbm_spec = pl.BlockSpec(memory_space=pl.ANY)
    vmem = pltpu.VMEM
    dma = pltpu.SemaphoreType.DMA
    return pl.pallas_call(
        layer_kernel,
        out_shape=(
            jax.ShapeDtypeStruct((BLK, HEADS * HEAD), BF16),
            jax.ShapeDtypeStruct((ROWS, D), BF16),
        ),
        in_specs=[hbm_spec] * 10,
        out_specs=(pl.BlockSpec(memory_space=vmem), pl.BlockSpec(memory_space=vmem)),
        scratch_shapes=[
            vmem((BLK, HEADS * HEAD), BF16),
            vmem((HEADS, BLK, HEAD), BF16),
            vmem((32, 2 * BLK, HEAD), BF16),
            vmem((HEADS * HEAD, D), BF16),
            vmem((1, D), F32),
            vmem((D, EFF), BF16),
            vmem((D, EFF), BF16),
            vmem((EFF, D), BF16),
            vmem((8, BLK), jnp.int32),
            vmem((8, BLK), F32),
            vmem((4, 16, BLK), F32),
            vmem((HEADS, BLK, HEAD), F32),
            vmem((HEADS, BLK, HEAD), F32),
            vmem((HEADS, BLK, HEAD), F32),
            vmem((BLK, D), F32),
            vmem((BLK, D), BF16),
            vmem((3, ROWS, D), BF16),
            vmem((ROWS, D), F32),
            vmem((4, 8 * SLOTS, BLK), BF16),
            vmem((4, BLK, 8 * SLOTS), BF16),
            vmem((16, CHUNKS, ROWS, WIDE), BF16),
            vmem((4, 8 * SLOTS, D), BF16),
            vmem((4, 8 * SLOTS, D), BF16),
            vmem((4, 8 * SLOTS, D), BF16),
            vmem((4, 8 * SLOTS, D), BF16),
            vmem((16, CHUNKS, ROWS, WIDE), F32),
            vmem((8, CHUNKS, ROWS, WIDE), BF16),
            vmem((7, CHUNKS, ROWS, WIDE), BF16),
            vmem((8, CHUNKS, ROWS, WIDE), BF16),
            vmem((7, CHUNKS, ROWS, WIDE), BF16),
            dma((10,)),
            dma((128,)),
            dma((3,)),
            dma((32,)),
            dma((4, 2)),
            dma((4,)),
            dma((4, 3)),
            dma((CHUNKS, 8)),
            dma((CHUNKS, 7)),
            dma((4, 8)),
            dma((4, 8)),
            dma((CHUNKS, 8)),
            dma((CHUNKS, 7)),
            dma((8,)),
        ],
        compiler_params=pltpu.CompilerParams(
            collective_id=0, has_side_effects=True, vmem_limit_bytes=53 * 1024 * 1024
        ),
        name="layer",
    )(
        queries, keys, values, out_weight, norm_gain.reshape(1, D),
        expert_gate.reshape(D, EFF), expert_up.reshape(D, EFF), expert_down.reshape(EFF, D),
        expert_ids.T, route_weights.T,
    )


def solution(mesh):
    in_specs = (
        P(("dp", "ctx"), "tp"),
        P(("dp", "ctx"), "tp"),
        P(("dp", "ctx"), "tp"),
        P("tp", None),
        P(),
        P(("ctx", "tp"), None, None),
        P(("ctx", "tp"), None, None),
        P(("ctx", "tp"), None, None),
        P(("dp", "ctx"), None),
        P(("dp", "ctx"), None),
    )
    out_specs = (P(("dp", "ctx"), "tp"), P(("dp", "ctx", "tp"), None))
    return jax.shard_map(
        per_device, mesh=mesh, in_specs=in_specs, out_specs=out_specs, check_vma=False
    )
```

```python
import math

import jax
import jax.numpy as jnp
from jax import lax
from jax.experimental import pallas as pl
from jax.experimental.pallas import tpu as pltpu
from jax.sharding import PartitionSpec as P

MESH = pl.DeviceIdType.MESH
BF16 = jnp.bfloat16
F32 = jnp.float32
HEAD = 128
HEADS = 8
BLK = 128
D = 2048
EFF = 384
ROWS = 32
SLOTS = 16
CHUNKS = 16
WIDE = D // CHUNKS
NEG = -1e30


def layer_kernel(
    q_hbm, k_hbm, v_hbm, w_hbm, gain_hbm, gate_hbm, up_hbm, down_hbm, ids_hbm, share_hbm,
    att_v, out_v,
    q_v, q_h, kv, w_v, gain_v, gate_v, up_v, down_v, ids_v, share_v, route,
    m_s, l_s, acc_s, proj_f, rs_s, rs_r, proj_own,
    dmap, mmap, xg, xs, xr, ys, ret, contrib, sp, sm, rp, rm,
    load_sem, send_sem, ring_send, kv_sem, kvz_sem, route_sem, rs_sem, agp_sem, agm_sem, xd_sem, xb_sem, rp_sem, rm_sem, self_sem,
):
    ctx = lax.axis_index("ctx")
    tp = lax.axis_index("tp")
    zh = ctx // 8
    row = ctx % 8
    x = row // 2
    core = ctx % 2
    z = zh * 4 + tp

    sends = []

    def send(src, dst, recv_sem, device):
        copy = pltpu.make_async_remote_copy(
            src_ref=src, dst_ref=dst, send_sem=send_sem.at[len(sends)], recv_sem=recv_sem,
            device_id=device, device_id_type=MESH,
        )
        copy.start()
        sends.append(copy)

    def arrived(dst, recv_sem):
        pltpu.make_async_remote_copy(
            src_ref=dst, dst_ref=dst, send_sem=send_sem.at[0], recv_sem=recv_sem,
            device_id=at_row(row), device_id_type=MESH,
        ).wait_recv()

    def at_zh(z_hi):
        return {"ctx": z_hi * 8 + row, "tp": tp}

    def at_row(r):
        return {"ctx": zh * 8 + r, "tp": tp}

    def at_z(zz):
        return {"ctx": (zz // 4) * 8 + row, "tp": zz % 4}

    def at_tp(t):
        return {"ctx": ctx, "tp": t}

    def zmod(offset):
        return (z + offset + 16) % 16

    loads = {}

    def load(name, src, dst):
        copy = pltpu.make_async_copy(src, dst, load_sem.at[len(loads)])
        copy.start()
        loads[name] = copy

    load("k", k_hbm, kv.at[ctx, pl.ds(0, BLK)])
    load("v", v_hbm, kv.at[ctx, pl.ds(BLK, BLK)])
    load("ids", ids_hbm, ids_v)
    load("share", share_hbm, share_v)
    load("q", q_hbm, q_v)
    load("w", w_hbm, w_v)
    load("gain", gain_hbm, gain_v)
    load("gate", gate_hbm, gate_v)
    load("up", up_hbm, up_v)
    load("down", down_hbm, down_v)

    barrier = pltpu.get_barrier_semaphore()
    partners = [at_zh((zh + d) % 4) for d in (1, 3)]
    partners += [at_row((row + o) % 8) for o in range(1, 8)]
    partners += [at_tp((tp + o) % 4) for o in (1, 2, 3)]
    above, below = at_z(zmod(1)), at_z(zmod(-1))
    partners += [above, below]
    for partner in partners:
        pl.semaphore_signal(barrier, inc=1, device_id=partner, device_id_type=MESH)

    loads["ids"].wait()
    loads["share"].wait()
    route[zh, 0:8, :] = ids_v[...].astype(F32)
    route[zh, 8:16, :] = share_v[...]
    loads["q"].wait()
    for h in range(HEADS):
        q_h[h] = q_v[:, h * HEAD : (h + 1) * HEAD]

    pl.semaphore_wait(barrier, len(partners))

    sibling = row + 1 - 2 * core
    loads["k"].wait()
    loads["v"].wait()

    def send_block(block, device):
        send(kv.at[block], kv.at[block], kv_sem.at[block], device)

    def x_row(dx):
        return ((x + dx) % 4) * 2 + core

    def half_block(z_hi, half):
        return kv.at[z_hi * 8 + row, pl.ds(half * BLK, BLK)]

    for half in range(2):
        for d in (1, 3):
            here = half_block(zh, half)
            send(here, here, kvz_sem.at[zh, half], at_zh((zh + d) % 4))
    for dx in (2, 1, 3):
        send_block(ctx, at_row(x_row(dx)))
    send_block(ctx, at_row(sibling))
    for d in (1, 3):
        send(route.at[zh], route.at[zh], route_sem.at[zh], at_zh((zh + d) % 4))

    score_scale = (HEAD**-0.5) * math.log2(math.e)

    def attend(s, first):
        def head(h, carry):
            keys = kv[pl.ds(s * 8, 8), 0:BLK, :].reshape(8 * BLK, HEAD)
            vals = kv[pl.ds(s * 8, 8), BLK : 2 * BLK, :].reshape(8 * BLK, HEAD)
            scores = lax.dot_general(
                q_h[h], keys, (((1,), (1,)), ((), ())), preferred_element_type=F32
            )
            scores = scores * score_scale
            if first:
                key_pos = lax.broadcasted_iota(jnp.int32, scores.shape, 1)
                query_pos = lax.broadcasted_iota(jnp.int32, scores.shape, 0) + row * BLK
                scores = jnp.where(key_pos <= query_pos, scores, NEG)
            top = jnp.max(scores, axis=1, keepdims=True)
            if first:
                new_max = jnp.broadcast_to(top, (BLK, HEAD))
            else:
                new_max = jnp.maximum(m_s[h], top)
            weights = [
                jnp.exp2(scores[:, j * HEAD : (j + 1) * HEAD] - new_max) for j in range(8)
            ]
            total = weights[0]
            for j in range(1, 8):
                total = total + weights[j]
            update = jnp.dot(
                jnp.concatenate([w.astype(BF16) for w in weights], axis=1),
                vals,
                preferred_element_type=F32,
            )
            if first:
                l_s[h] = total
                acc_s[h] = update
            else:
                rescale = jnp.exp2(m_s[h] - new_max)
                l_s[h] = l_s[h] * rescale + total
                acc_s[h] = acc_s[h] * rescale + update
            m_s[h] = new_max
            return carry

        lax.fori_loop(0, HEADS, head, 0, unroll=2)

    def collect(s):
        for dx in (1, 3, 2):
            block = s * 8 + x_row(dx)
            arrived(kv.at[block], kv_sem.at[block])
            send_block(block, at_row(sibling))
        for dx in (0, 1, 3, 2):
            block = s * 8 + ((x + dx) % 4) * 2 + 1 - core
            arrived(kv.at[block], kv_sem.at[block])

    collect(zh)
    attend(zh, True)

    def spread(block):
        for dx in (2, 1, 3):
            send_block(block, at_row(x_row(dx)))
        send_block(block, at_row(sibling))

    passed = (zh + 3 + 2 * core) % 4
    other = (zh + 1 + 2 * core) % 4
    for half in range(2):
        here = half_block(passed, half)
        arrived(here, kvz_sem.at[passed, half])
        send(here, here, kvz_sem.at[passed, half], at_zh(other))
    for half in range(2):
        arrived(half_block(other, half), kvz_sem.at[other, half])
    for d in (3, 1):
        spread(((zh + d) % 4) * 8 + row)
    for d in (3, 1):
        src = (zh + d) % 4
        arrived(route.at[src], route_sem.at[src])
    src = (zh + 3) % 4
    send(route.at[src], route.at[src], route_sem.at[src], at_zh((zh + 1) % 4))

    def attend_earlier(d):
        s = (zh + d) % 4
        collect(s)

        @pl.when(s < zh)
        def _():
            attend(s, False)

    attend_earlier(3)
    far = (zh + 2) % 4
    for half in range(2):
        arrived(half_block(far, half), kvz_sem.at[far, half])
    spread(far * 8 + row)
    attend_earlier(1)

    src = (zh + 2) % 4
    arrived(route.at[src], route_sem.at[src])
    earlier = (
        lax.broadcasted_iota(jnp.int32, (BLK, BLK), 0)
        < lax.broadcasted_iota(jnp.int32, (BLK, BLK), 1)
    ).astype(F32).astype(BF16)
    slot = lax.broadcasted_iota(jnp.int32, (SLOTS, BLK), 0).astype(F32)
    for b in range(4):
        ids = route[b, 0:8, :]
        share = route[b, 8:16, :]
        share = share / jnp.sum(share, axis=0, keepdims=True)
        hits, picked = [], []
        for r in range(8):
            same = ids == (zh * 32 + tp + 4 * r).astype(F32)
            hits.append(jnp.sum(jnp.where(same, 1.0, 0.0), axis=0, keepdims=True))
            picked.append(jnp.sum(jnp.where(same, share, 0.0), axis=0, keepdims=True))
        hit = jnp.concatenate(hits, axis=0)
        rank = jnp.dot(hit.astype(BF16), earlier, preferred_element_type=F32)
        choose = [
            jnp.where(slot == rank[r : r + 1], hit[r : r + 1], 0.0) for r in range(8)
        ]
        dmap[b] = jnp.concatenate(choose, axis=0).astype(BF16)
        back = jnp.concatenate([choose[r] * picked[r] for r in range(8)], axis=0)
        mmap[b] = back.T.astype(BF16)

    attend_earlier(2)

    for h in range(HEADS):
        att_v[:, h * HEAD : (h + 1) * HEAD] = (
            acc_s[h] / jnp.sum(l_s[h], axis=1, keepdims=True)
        ).astype(BF16)

    loads["w"].wait()
    for n in range(4):
        cols = pl.ds(n * 512, 512)
        part = jnp.dot(att_v[...], w_v[:, cols], preferred_element_type=F32)
        proj_f[:, cols] = part
        rs_s[:, cols] = part.astype(BF16)
        for o in (2, 1, 3):
            owner = (tp + o) % 4
            send(
                rs_s.at[pl.ds(pl.multiple_of(owner * ROWS, ROWS), ROWS), cols],
                rs_r.at[o - 1, :, cols],
                rs_sem.at[n, o - 1],
                at_tp(owner),
            )
    loads["gain"].wait()
    for n in range(4):
        cols = pl.ds(n * 512, 512)
        for o in (2, 1, 3):
            arrived(rs_r.at[o - 1, :, cols], rs_sem.at[n, o - 1])
    own_rows = pl.ds(pl.multiple_of(tp * ROWS, ROWS), ROWS)
    projected = (
        proj_f[own_rows, :] + rs_r[0].astype(F32) + rs_r[1].astype(F32) + rs_r[2].astype(F32)
    )
    proj_own[...] = projected
    inverse = lax.rsqrt(jnp.mean(projected * projected, axis=1, keepdims=True) + 1e-06)
    normed = (projected * inverse * gain_v[...]).astype(BF16)
    for j in range(CHUNKS):
        xg[z, j] = normed[:, j * WIDE : (j + 1) * WIDE]

    def pass_on(src, dst, sems, send_at, j, k, device):
        pltpu.make_async_remote_copy(
            src_ref=src, dst_ref=dst, send_sem=ring_send.at[send_at], recv_sem=sems.at[j, k - 1],
            device_id=device, device_id_type=MESH,
        ).start()

    def ring_step(k):
        def chunk(j, carry):
            here = xg.at[zmod(1 - k), j]
            if k > 1:
                arrived(here, agp_sem.at[j, k - 2])
            pass_on(here, here, agp_sem, 0, j, k, above)
            here = xg.at[zmod(k - 1), j]
            if k > 1:
                arrived(here, agm_sem.at[j, k - 2])
            if k <= 7:
                pass_on(here, here, agm_sem, 0, j, k, below)
            return carry

        lax.fori_loop(0, CHUNKS, chunk, 0)

    def ring_end():
        def chunk(j, carry):
            arrived(xg.at[zmod(-8), j], agp_sem.at[j, 7])
            return carry

        lax.fori_loop(0, CHUNKS, chunk, 0)

    side = 2 * (tp // 2) - 1
    order = [zh, (zh + side + 4) % 4, (zh - side + 4) % 4, (zh + 2) % 4]
    own_slots = pl.ds(pl.multiple_of(row * SLOTS, SLOTS), SLOTS)
    local = {}

    def exchange(src, dst, sems, i, n):
        for o in (4, 5, 3, 2, 6, 7, 1):
            r = (row + o) % 8
            slots = pl.ds(pl.multiple_of(r * SLOTS, SLOTS), SLOTS)
            send(src.at[i, slots], dst.at[i, own_slots], sems.at[i, o], at_row(r))
        copy = pltpu.make_async_copy(
            src.at[i, own_slots], dst.at[i, own_slots], self_sem.at[n]
        )
        copy.start()
        local[n] = copy

    def exchanged(dst, sems, i, copy):
        for o in range(1, 8):
            r = (row - o + 8) % 8
            slots = pl.ds(pl.multiple_of(r * SLOTS, SLOTS), SLOTS)
            arrived(dst.at[i, slots], sems.at[i, o])
        copy.wait()

    def dispatch(i):
        for n in range(4):
            cols = pl.ds(n * 512, 512)
            tokens = [
                xg[pl.ds(order[i] * 4, 4), j].reshape(BLK, WIDE)
                for j in range(n * 512 // WIDE, (n + 1) * 512 // WIDE)
            ]
            xs[i, :, cols] = jnp.dot(
                dmap[order[i]], jnp.concatenate(tokens, axis=1), preferred_element_type=F32
            ).astype(BF16)
        exchange(xs, xr, xd_sem, i, i)

    def expert(i):
        exchanged(xr, xd_sem, i, local[i])
        items = xr[i]
        gate = jnp.dot(items, gate_v[...], preferred_element_type=F32)
        up = jnp.dot(items, up_v[...], preferred_element_type=F32)
        act = (gate / (1.0 + jnp.exp(-gate)) * up).astype(BF16)
        for n in range(4):
            cols = pl.ds(n * 512, 512)
            ys[i, :, cols] = jnp.dot(
                act, down_v[:, cols], preferred_element_type=F32
            ).astype(BF16)
        exchange(ys, ret, xb_sem, i, 4 + i)

    def mix(i):
        exchanged(ret, xb_sem, i, local[4 + i])
        for n in range(4):
            cols = pl.ds(n * 512, 512)
            mixed = jnp.dot(mmap[order[i]], ret[i, :, cols], preferred_element_type=F32)
            for j in range(512 // WIDE):
                contrib[pl.ds(order[i] * 4, 4), n * 512 // WIDE + j] = mixed[
                    :, j * WIDE : (j + 1) * WIDE
                ].reshape(4, ROWS, WIDE)

    for k in (1, 2, 3, 4):
        ring_step(k)
    dispatch(0)
    for k in (5, 6):
        ring_step(k)
    dispatch(1)
    ring_step(7)
    loads["gate"].wait()
    loads["up"].wait()
    loads["down"].wait()
    expert(0)
    ring_step(8)
    dispatch(2)
    expert(1)
    ring_end()
    dispatch(3)
    expert(2)
    mix(0)
    mix(1)
    expert(3)
    mix(2)
    mix(3)

    def scatter_step(k):
        def chunk(j, carry):
            total = contrib[zmod(9 - k), j]
            if k > 1:
                arrived(rp.at[k - 2, j], rp_sem.at[j, k - 2])
                total = total + rp[k - 2, j].astype(F32)
            sp[k - 1, j] = total.astype(BF16)
            pass_on(sp.at[k - 1, j], rp.at[k - 1, j], rp_sem, 1, j, k, above)
            if k <= 7:
                total = contrib[zmod(k - 8), j]
                if k > 1:
                    arrived(rm.at[k - 2, j], rm_sem.at[j, k - 2])
                    total = total + rm[k - 2, j].astype(F32)
                sm[k - 1, j] = total.astype(BF16)
                pass_on(sm.at[k - 1, j], rm.at[k - 1, j], rm_sem, 2, j, k, below)
            return carry

        lax.fori_loop(0, CHUNKS, chunk, 0)

    for k in range(1, 9):
        scatter_step(k)
    for j in range(CHUNKS):
        cols = pl.ds(j * WIDE, WIDE)
        arrived(rm.at[6, j], rm_sem.at[j, 6])
        arrived(rp.at[7, j], rp_sem.at[j, 7])
        out_v[:, cols] = (
            proj_own[:, cols]
            + contrib[z, j]
            + rp[7, j].astype(F32)
            + rm[6, j].astype(F32)
        ).astype(BF16)
    for i, sent in enumerate((xg.at[pl.ds(0, 15)], sp, sm)):
        pltpu.make_async_remote_copy(
            src_ref=sent, dst_ref=sent, send_sem=ring_send.at[i], recv_sem=ring_send.at[i],
            device_id=above, device_id_type=MESH,
        ).wait_send()
    for copy in sends:
        copy.wait_send()


def per_device(
    queries, keys, values, out_weight, norm_gain,
    expert_gate, expert_up, expert_down, expert_ids, route_weights,
):
    hbm_spec = pl.BlockSpec(memory_space=pl.ANY)
    vmem = pltpu.VMEM
    dma = pltpu.SemaphoreType.DMA
    pinned = [
        pltpu.with_memory_space_constraint(operand, pltpu.HBM)
        for operand in (
            queries, keys, values, out_weight, norm_gain.reshape(1, D),
            expert_gate.reshape(D, EFF), expert_up.reshape(D, EFF), expert_down.reshape(EFF, D),
            expert_ids.T, route_weights.T,
        )
    ]
    return pl.pallas_call(
        layer_kernel,
        out_shape=(
            jax.ShapeDtypeStruct((BLK, HEADS * HEAD), BF16),
            jax.ShapeDtypeStruct((ROWS, D), BF16),
        ),
        in_specs=[hbm_spec] * 10,
        out_specs=(pl.BlockSpec(memory_space=vmem), pl.BlockSpec(memory_space=vmem)),
        scratch_shapes=[
            vmem((BLK, HEADS * HEAD), BF16),
            vmem((HEADS, BLK, HEAD), BF16),
            vmem((32, 2 * BLK, HEAD), BF16),
            vmem((HEADS * HEAD, D), BF16),
            vmem((1, D), F32),
            vmem((D, EFF), BF16),
            vmem((D, EFF), BF16),
            vmem((EFF, D), BF16),
            vmem((8, BLK), jnp.int32),
            vmem((8, BLK), F32),
            vmem((4, 16, BLK), F32),
            vmem((HEADS, BLK, HEAD), F32),
            vmem((HEADS, BLK, HEAD), F32),
            vmem((HEADS, BLK, HEAD), F32),
            vmem((BLK, D), F32),
            vmem((BLK, D), BF16),
            vmem((3, ROWS, D), BF16),
            vmem((ROWS, D), F32),
            vmem((4, 8 * SLOTS, BLK), BF16),
            vmem((4, BLK, 8 * SLOTS), BF16),
            vmem((16, CHUNKS, ROWS, WIDE), BF16),
            vmem((4, 8 * SLOTS, D), BF16),
            vmem((4, 8 * SLOTS, D), BF16),
            vmem((4, 8 * SLOTS, D), BF16),
            vmem((4, 8 * SLOTS, D), BF16),
            vmem((16, CHUNKS, ROWS, WIDE), F32),
            vmem((8, CHUNKS, ROWS, WIDE), BF16),
            vmem((7, CHUNKS, ROWS, WIDE), BF16),
            vmem((8, CHUNKS, ROWS, WIDE), BF16),
            vmem((7, CHUNKS, ROWS, WIDE), BF16),
            dma((10,)),
            dma((128,)),
            dma((3,)),
            dma((32,)),
            dma((4, 2)),
            dma((4,)),
            dma((4, 3)),
            dma((CHUNKS, 8)),
            dma((CHUNKS, 7)),
            dma((4, 8)),
            dma((4, 8)),
            dma((CHUNKS, 8)),
            dma((CHUNKS, 7)),
            dma((8,)),
        ],
        compiler_params=pltpu.CompilerParams(
            collective_id=0, has_side_effects=True, vmem_limit_bytes=53 * 1024 * 1024
        ),
        name="layer",
    )(*pinned)


def solution(mesh):
    in_specs = (
        P(("dp", "ctx"), "tp"),
        P(("dp", "ctx"), "tp"),
        P(("dp", "ctx"), "tp"),
        P("tp", None),
        P(),
        P(("ctx", "tp"), None, None),
        P(("ctx", "tp"), None, None),
        P(("ctx", "tp"), None, None),
        P(("dp", "ctx"), None),
        P(("dp", "ctx"), None),
    )
    out_specs = (P(("dp", "ctx"), "tp"), P(("dp", "ctx", "tp"), None))
    return jax.shard_map(
        per_device, mesh=mesh, in_specs=in_specs, out_specs=out_specs, check_vma=False
    )
```

```python
import math

import jax
import jax.numpy as jnp
from jax import lax
from jax.experimental import pallas as pl
from jax.experimental.pallas import tpu as pltpu
from jax.sharding import PartitionSpec as P

MESH = pl.DeviceIdType.MESH
BF16 = jnp.bfloat16
F32 = jnp.float32
HEAD = 128
HEADS = 8
BLK = 128
D = 2048
EFF = 384
ROWS = 32
SLOTS = 16
CHUNKS = 16
WIDE = D // CHUNKS
NEG = -1e30


def layer_kernel(
    q_hbm, k_hbm, v_hbm, w_hbm, gain_hbm, gate_hbm, up_hbm, down_hbm, ids_hbm, share_hbm,
    att_v, out_v,
    q_v, q_h, kv, w_v, gain_v, gate_v, up_v, down_v, ids_v, share_v, route,
    m_s, l_s, acc_s, proj_f, rs_s, rs_r, proj_own,
    dmap, mmap, xg, xs, xr, ys, ret, contrib, sp, sm, rp, rm,
    load_sem, send_sem, ring_send, kv_sem, kvz_sem, route_sem, rs_sem, agp_sem, agm_sem, xd_sem, xb_sem, rp_sem, rm_sem, self_sem,
):
    ctx = lax.axis_index("ctx")
    tp = lax.axis_index("tp")
    zh = ctx // 8
    row = ctx % 8
    x = row // 2
    core = ctx % 2
    z = zh * 4 + tp

    sends = []

    def send(src, dst, recv_sem, device):
        copy = pltpu.make_async_remote_copy(
            src_ref=src, dst_ref=dst, send_sem=send_sem.at[len(sends)], recv_sem=recv_sem,
            device_id=device, device_id_type=MESH,
        )
        copy.start()
        sends.append(copy)

    def arrived(dst, recv_sem):
        pltpu.make_async_remote_copy(
            src_ref=dst, dst_ref=dst, send_sem=send_sem.at[0], recv_sem=recv_sem,
            device_id=at_row(row), device_id_type=MESH,
        ).wait_recv()

    def at_zh(z_hi):
        return {"ctx": z_hi * 8 + row, "tp": tp}

    def at_row(r):
        return {"ctx": zh * 8 + r, "tp": tp}

    def at_z(zz):
        return {"ctx": (zz // 4) * 8 + row, "tp": zz % 4}

    def at_tp(t):
        return {"ctx": ctx, "tp": t}

    def zmod(offset):
        return (z + offset + 16) % 16

    loads = {}

    def load(name, src, dst):
        copy = pltpu.make_async_copy(src, dst, load_sem.at[len(loads)])
        copy.start()
        loads[name] = copy

    load("k", k_hbm, kv.at[ctx, pl.ds(0, BLK)])
    load("v", v_hbm, kv.at[ctx, pl.ds(BLK, BLK)])
    load("ids", ids_hbm, ids_v)
    load("share", share_hbm, share_v)
    load("q", q_hbm, q_v)
    load("w", w_hbm, w_v)
    load("gain", gain_hbm, gain_v)
    load("gate", gate_hbm, gate_v)
    load("up", up_hbm, up_v)
    load("down", down_hbm, down_v)

    barrier = pltpu.get_barrier_semaphore()
    partners = [at_zh((zh + d) % 4) for d in (1, 3)]
    partners += [at_row((row + o) % 8) for o in range(1, 8)]
    partners += [at_tp((tp + o) % 4) for o in (1, 2, 3)]
    above, below = at_z(zmod(1)), at_z(zmod(-1))
    partners += [above, below]
    for partner in partners:
        pl.semaphore_signal(barrier, inc=1, device_id=partner, device_id_type=MESH)

    loads["ids"].wait()
    loads["share"].wait()
    route[zh, 0:8, :] = ids_v[...].astype(F32)
    route[zh, 8:16, :] = share_v[...]
    loads["q"].wait()
    for h in range(HEADS):
        q_h[h] = q_v[:, h * HEAD : (h + 1) * HEAD]

    pl.semaphore_wait(barrier, len(partners))

    sibling = row + 1 - 2 * core
    loads["k"].wait()
    loads["v"].wait()

    def send_block(block, device):
        send(kv.at[block], kv.at[block], kv_sem.at[block], device)

    def x_row(dx):
        return ((x + dx) % 4) * 2 + core

    def half_block(z_hi, half):
        return kv.at[z_hi * 8 + row, pl.ds(half * BLK, BLK)]

    for half in range(2):
        for d in (1, 3):
            here = half_block(zh, half)
            send(here, here, kvz_sem.at[zh, half], at_zh((zh + d) % 4))
    for dx in (2, 1, 3):
        send_block(ctx, at_row(x_row(dx)))
    send_block(ctx, at_row(sibling))
    for d in (1, 3):
        send(route.at[zh], route.at[zh], route_sem.at[zh], at_zh((zh + d) % 4))

    score_scale = (HEAD**-0.5) * math.log2(math.e)

    def attend(s, first):
        def head(h, carry):
            keys = kv[pl.ds(s * 8, 8), 0:BLK, :].reshape(8 * BLK, HEAD)
            vals = kv[pl.ds(s * 8, 8), BLK : 2 * BLK, :].reshape(8 * BLK, HEAD)
            scores = lax.dot_general(
                q_h[h], keys, (((1,), (1,)), ((), ())), preferred_element_type=F32
            )
            scores = scores * score_scale
            if first:
                key_pos = lax.broadcasted_iota(jnp.int32, scores.shape, 1)
                query_pos = lax.broadcasted_iota(jnp.int32, scores.shape, 0) + row * BLK
                scores = jnp.where(key_pos <= query_pos, scores, NEG)
            top = jnp.max(scores, axis=1, keepdims=True)
            if first:
                new_max = jnp.broadcast_to(top, (BLK, HEAD))
            else:
                new_max = jnp.maximum(m_s[h], top)
            weights = [
                jnp.exp2(scores[:, j * HEAD : (j + 1) * HEAD] - new_max) for j in range(8)
            ]
            total = weights[0]
            for j in range(1, 8):
                total = total + weights[j]
            update = jnp.dot(
                jnp.concatenate([w.astype(BF16) for w in weights], axis=1),
                vals,
                preferred_element_type=F32,
            )
            if first:
                l_s[h] = total
                acc_s[h] = update
            else:
                rescale = jnp.exp2(m_s[h] - new_max)
                l_s[h] = l_s[h] * rescale + total
                acc_s[h] = acc_s[h] * rescale + update
            m_s[h] = new_max
            return carry

        lax.fori_loop(0, HEADS, head, 0, unroll=4)

    def collect(s):
        for dx in (1, 3, 2):
            block = s * 8 + x_row(dx)
            arrived(kv.at[block], kv_sem.at[block])
            send_block(block, at_row(sibling))
        for dx in (0, 1, 3, 2):
            block = s * 8 + ((x + dx) % 4) * 2 + 1 - core
            arrived(kv.at[block], kv_sem.at[block])

    collect(zh)
    attend(zh, True)

    def spread(block):
        for dx in (2, 1, 3):
            send_block(block, at_row(x_row(dx)))
        send_block(block, at_row(sibling))

    passed = (zh + 3 + 2 * core) % 4
    other = (zh + 1 + 2 * core) % 4
    for half in range(2):
        here = half_block(passed, half)
        arrived(here, kvz_sem.at[passed, half])
        send(here, here, kvz_sem.at[passed, half], at_zh(other))
    for half in range(2):
        arrived(half_block(other, half), kvz_sem.at[other, half])
    for d in (3, 1):
        spread(((zh + d) % 4) * 8 + row)
    for d in (3, 1):
        src = (zh + d) % 4
        arrived(route.at[src], route_sem.at[src])
    src = (zh + 3) % 4
    send(route.at[src], route.at[src], route_sem.at[src], at_zh((zh + 1) % 4))

    def attend_earlier(d):
        s = (zh + d) % 4
        collect(s)

        @pl.when(s < zh)
        def _():
            attend(s, False)

    attend_earlier(3)
    far = (zh + 2) % 4
    for half in range(2):
        arrived(half_block(far, half), kvz_sem.at[far, half])
    spread(far * 8 + row)
    attend_earlier(1)

    attend_earlier(2)

    for h in range(HEADS):
        att_v[:, h * HEAD : (h + 1) * HEAD] = (
            acc_s[h] / jnp.sum(l_s[h], axis=1, keepdims=True)
        ).astype(BF16)

    loads["w"].wait()
    for n in range(4):
        cols = pl.ds(n * 512, 512)
        part = jnp.dot(att_v[...], w_v[:, cols], preferred_element_type=F32)
        proj_f[:, cols] = part
        rs_s[:, cols] = part.astype(BF16)
        for o in (2, 1, 3):
            owner = (tp + o) % 4
            send(
                rs_s.at[pl.ds(pl.multiple_of(owner * ROWS, ROWS), ROWS), cols],
                rs_r.at[o - 1, :, cols],
                rs_sem.at[n, o - 1],
                at_tp(owner),
            )
    src = (zh + 2) % 4
    arrived(route.at[src], route_sem.at[src])
    earlier = (
        lax.broadcasted_iota(jnp.int32, (BLK, BLK), 0)
        < lax.broadcasted_iota(jnp.int32, (BLK, BLK), 1)
    ).astype(F32).astype(BF16)
    slot = lax.broadcasted_iota(jnp.int32, (SLOTS, BLK), 0).astype(F32)
    for b in range(4):
        ids = route[b, 0:8, :]
        share = route[b, 8:16, :]
        share = share / jnp.sum(share, axis=0, keepdims=True)
        hits, picked = [], []
        for r in range(8):
            same = ids == (zh * 32 + tp + 4 * r).astype(F32)
            hits.append(jnp.sum(jnp.where(same, 1.0, 0.0), axis=0, keepdims=True))
            picked.append(jnp.sum(jnp.where(same, share, 0.0), axis=0, keepdims=True))
        hit = jnp.concatenate(hits, axis=0)
        rank = jnp.dot(hit.astype(BF16), earlier, preferred_element_type=F32)
        choose = [
            jnp.where(slot == rank[r : r + 1], hit[r : r + 1], 0.0) for r in range(8)
        ]
        dmap[b] = jnp.concatenate(choose, axis=0).astype(BF16)
        back = jnp.concatenate([choose[r] * picked[r] for r in range(8)], axis=0)
        mmap[b] = back.T.astype(BF16)

    loads["gain"].wait()
    for n in range(4):
        cols = pl.ds(n * 512, 512)
        for o in (2, 1, 3):
            arrived(rs_r.at[o - 1, :, cols], rs_sem.at[n, o - 1])
    own_rows = pl.ds(pl.multiple_of(tp * ROWS, ROWS), ROWS)
    projected = (
        proj_f[own_rows, :] + rs_r[0].astype(F32) + rs_r[1].astype(F32) + rs_r[2].astype(F32)
    )
    proj_own[...] = projected
    inverse = lax.rsqrt(jnp.mean(projected * projected, axis=1, keepdims=True) + 1e-06)
    normed = (projected * inverse * gain_v[...]).astype(BF16)
    for j in range(CHUNKS):
        xg[z, j] = normed[:, j * WIDE : (j + 1) * WIDE]

    def pass_on(src, dst, sems, send_at, j, k, device):
        pltpu.make_async_remote_copy(
            src_ref=src, dst_ref=dst, send_sem=ring_send.at[send_at], recv_sem=sems.at[j, k - 1],
            device_id=device, device_id_type=MESH,
        ).start()

    def ring_step(k):
        def chunk(j, carry):
            here = xg.at[zmod(1 - k), j]
            if k > 1:
                arrived(here, agp_sem.at[j, k - 2])
            pass_on(here, here, agp_sem, 0, j, k, above)
            here = xg.at[zmod(k - 1), j]
            if k > 1:
                arrived(here, agm_sem.at[j, k - 2])
            if k <= 7:
                pass_on(here, here, agm_sem, 0, j, k, below)
            return carry

        lax.fori_loop(0, CHUNKS, chunk, 0)

    def ring_end():
        def chunk(j, carry):
            arrived(xg.at[zmod(-8), j], agp_sem.at[j, 7])
            return carry

        lax.fori_loop(0, CHUNKS, chunk, 0)

    side = 2 * (tp // 2) - 1
    order = [zh, (zh + side + 4) % 4, (zh - side + 4) % 4, (zh + 2) % 4]
    own_slots = pl.ds(pl.multiple_of(row * SLOTS, SLOTS), SLOTS)
    local = {}

    def exchange(src, dst, sems, i, n):
        for o in (4, 5, 3, 2, 6, 7, 1):
            r = (row + o) % 8
            slots = pl.ds(pl.multiple_of(r * SLOTS, SLOTS), SLOTS)
            send(src.at[i, slots], dst.at[i, own_slots], sems.at[i, o], at_row(r))
        copy = pltpu.make_async_copy(
            src.at[i, own_slots], dst.at[i, own_slots], self_sem.at[n]
        )
        copy.start()
        local[n] = copy

    def exchanged(dst, sems, i, copy):
        for o in range(1, 8):
            r = (row - o + 8) % 8
            slots = pl.ds(pl.multiple_of(r * SLOTS, SLOTS), SLOTS)
            arrived(dst.at[i, slots], sems.at[i, o])
        copy.wait()

    def dispatch(i):
        for n in range(4):
            cols = pl.ds(n * 512, 512)
            tokens = [
                xg[pl.ds(order[i] * 4, 4), j].reshape(BLK, WIDE)
                for j in range(n * 512 // WIDE, (n + 1) * 512 // WIDE)
            ]
            xs[i, :, cols] = jnp.dot(
                dmap[order[i]], jnp.concatenate(tokens, axis=1), preferred_element_type=F32
            ).astype(BF16)
        exchange(xs, xr, xd_sem, i, i)

    def expert(i):
        exchanged(xr, xd_sem, i, local[i])
        items = xr[i]
        gate = jnp.dot(items, gate_v[...], preferred_element_type=F32)
        up = jnp.dot(items, up_v[...], preferred_element_type=F32)
        act = (gate / (1.0 + jnp.exp(-gate)) * up).astype(BF16)
        for n in range(4):
            cols = pl.ds(n * 512, 512)
            ys[i, :, cols] = jnp.dot(
                act, down_v[:, cols], preferred_element_type=F32
            ).astype(BF16)
        exchange(ys, ret, xb_sem, i, 4 + i)

    def mix(i):
        exchanged(ret, xb_sem, i, local[4 + i])
        for n in range(4):
            cols = pl.ds(n * 512, 512)
            mixed = jnp.dot(mmap[order[i]], ret[i, :, cols], preferred_element_type=F32)
            for j in range(512 // WIDE):
                contrib[pl.ds(order[i] * 4, 4), n * 512 // WIDE + j] = mixed[
                    :, j * WIDE : (j + 1) * WIDE
                ].reshape(4, ROWS, WIDE)

    for k in (1, 2, 3, 4):
        ring_step(k)
    dispatch(0)
    for k in (5, 6):
        ring_step(k)
    dispatch(1)
    ring_step(7)
    loads["gate"].wait()
    loads["up"].wait()
    loads["down"].wait()
    expert(0)
    ring_step(8)
    dispatch(2)
    expert(1)
    ring_end()
    dispatch(3)
    expert(2)
    mix(0)
    mix(1)
    expert(3)
    mix(2)
    mix(3)

    def scatter_step(k):
        def chunk(j, carry):
            total = contrib[zmod(9 - k), j]
            if k > 1:
                arrived(rp.at[k - 2, j], rp_sem.at[j, k - 2])
                total = total + rp[k - 2, j].astype(F32)
            sp[k - 1, j] = total.astype(BF16)
            pass_on(sp.at[k - 1, j], rp.at[k - 1, j], rp_sem, 1, j, k, above)
            if k <= 7:
                total = contrib[zmod(k - 8), j]
                if k > 1:
                    arrived(rm.at[k - 2, j], rm_sem.at[j, k - 2])
                    total = total + rm[k - 2, j].astype(F32)
                sm[k - 1, j] = total.astype(BF16)
                pass_on(sm.at[k - 1, j], rm.at[k - 1, j], rm_sem, 2, j, k, below)
            return carry

        lax.fori_loop(0, CHUNKS, chunk, 0)

    for k in range(1, 9):
        scatter_step(k)
    for j in range(CHUNKS):
        cols = pl.ds(j * WIDE, WIDE)
        arrived(rm.at[6, j], rm_sem.at[j, 6])
        arrived(rp.at[7, j], rp_sem.at[j, 7])
        out_v[:, cols] = (
            proj_own[:, cols]
            + contrib[z, j]
            + rp[7, j].astype(F32)
            + rm[6, j].astype(F32)
        ).astype(BF16)
    for i, sent in enumerate((xg.at[pl.ds(0, 15)], sp, sm)):
        pltpu.make_async_remote_copy(
            src_ref=sent, dst_ref=sent, send_sem=ring_send.at[i], recv_sem=ring_send.at[i],
            device_id=above, device_id_type=MESH,
        ).wait_send()
    for copy in sends:
        copy.wait_send()


def per_device(
    queries, keys, values, out_weight, norm_gain,
    expert_gate, expert_up, expert_down, expert_ids, route_weights,
):
    hbm_spec = pl.BlockSpec(memory_space=pl.ANY)
    vmem = pltpu.VMEM
    dma = pltpu.SemaphoreType.DMA
    pinned = [
        pltpu.with_memory_space_constraint(operand, pltpu.HBM)
        for operand in (
            queries, keys, values, out_weight, norm_gain.reshape(1, D),
            expert_gate.reshape(D, EFF), expert_up.reshape(D, EFF), expert_down.reshape(EFF, D),
            expert_ids.T, route_weights.T,
        )
    ]
    return pl.pallas_call(
        layer_kernel,
        out_shape=(
            jax.ShapeDtypeStruct((BLK, HEADS * HEAD), BF16),
            jax.ShapeDtypeStruct((ROWS, D), BF16),
        ),
        in_specs=[hbm_spec] * 10,
        out_specs=(pl.BlockSpec(memory_space=vmem), pl.BlockSpec(memory_space=vmem)),
        scratch_shapes=[
            vmem((BLK, HEADS * HEAD), BF16),
            vmem((HEADS, BLK, HEAD), BF16),
            vmem((32, 2 * BLK, HEAD), BF16),
            vmem((HEADS * HEAD, D), BF16),
            vmem((1, D), F32),
            vmem((D, EFF), BF16),
            vmem((D, EFF), BF16),
            vmem((EFF, D), BF16),
            vmem((8, BLK), jnp.int32),
            vmem((8, BLK), F32),
            vmem((4, 16, BLK), F32),
            vmem((HEADS, BLK, HEAD), F32),
            vmem((HEADS, BLK, HEAD), F32),
            vmem((HEADS, BLK, HEAD), F32),
            vmem((BLK, D), F32),
            vmem((BLK, D), BF16),
            vmem((3, ROWS, D), BF16),
            vmem((ROWS, D), F32),
            vmem((4, 8 * SLOTS, BLK), BF16),
            vmem((4, BLK, 8 * SLOTS), BF16),
            vmem((16, CHUNKS, ROWS, WIDE), BF16),
            vmem((4, 8 * SLOTS, D), BF16),
            vmem((4, 8 * SLOTS, D), BF16),
            vmem((4, 8 * SLOTS, D), BF16),
            vmem((4, 8 * SLOTS, D), BF16),
            vmem((16, CHUNKS, ROWS, WIDE), F32),
            vmem((8, CHUNKS, ROWS, WIDE), BF16),
            vmem((7, CHUNKS, ROWS, WIDE), BF16),
            vmem((8, CHUNKS, ROWS, WIDE), BF16),
            vmem((7, CHUNKS, ROWS, WIDE), BF16),
            dma((10,)),
            dma((128,)),
            dma((3,)),
            dma((32,)),
            dma((4, 2)),
            dma((4,)),
            dma((4, 3)),
            dma((CHUNKS, 8)),
            dma((CHUNKS, 7)),
            dma((4, 8)),
            dma((4, 8)),
            dma((CHUNKS, 8)),
            dma((CHUNKS, 7)),
            dma((8,)),
        ],
        compiler_params=pltpu.CompilerParams(
            collective_id=0, has_side_effects=True, vmem_limit_bytes=53 * 1024 * 1024
        ),
        name="layer",
    )(*pinned)


def solution(mesh):
    in_specs = (
        P(("dp", "ctx"), "tp"),
        P(("dp", "ctx"), "tp"),
        P(("dp", "ctx"), "tp"),
        P("tp", None),
        P(),
        P(("ctx", "tp"), None, None),
        P(("ctx", "tp"), None, None),
        P(("ctx", "tp"), None, None),
        P(("dp", "ctx"), None),
        P(("dp", "ctx"), None),
    )
    out_specs = (P(("dp", "ctx"), "tp"), P(("dp", "ctx", "tp"), None))
    return jax.shard_map(
        per_device, mesh=mesh, in_specs=in_specs, out_specs=out_specs, check_vma=False
    )
```
